768 devices in a mesh: dom: 192 (over z, y, core), sub: 4 (over x).
Axes of the slice: x: 4, y: 8, z: 12, core: 2. Of those that a mesh axis runs over, the one named last changes fastest.
Arguments:
- wavefield: float32 [9, 35, 344064], P(None, None, ('dom', 'sub')), may hold values from -6 to 6
- material: float32 [3, 344064], P(None, ('dom', 'sub')), may hold values from 0.5 to 4
- geometry: float32 [3, 3, 344064], P(None, None, ('dom', 'sub')), may hold values from -4 to 4
- face_scale: float32 [4, 344064], P(None, ('dom', 'sub')), may hold values from 0.5 to 2
- derivative: float32 [3, 35, 35], replicated, may hold values from -1 to 1
- lift_matrix: float32 [35, 60], replicated, may hold values from -0.75 to 0.75
- neighbour: int32 [4, 344064], P(None, ('dom', 'sub')), may hold values from 0 to 1343, as said below
- orient: int32 [4, 344064], P(None, ('dom', 'sub')), may hold values from 0 to 2
- halo_faces: int32 [2, 172032], P(None, ('dom', 'sub')), may hold values from 0 to 1023, as said below
- interface_send: int32 [2, 3, 24576], P(None, None, ('dom', 'sub')), may hold values from 0 to 1023, as said below
Outputs:
- new_wavefield: float32 [9, 35, 344064], P(None, None, ('dom', 'sub'))
The draws below stay inside these ranges and needn't reach their ends.
Inputs may be any that keep to these rules, and one draw needn't show every extreme that they name: `neighbour`: for a face of a partition's cluster with E elements, the entry names a column of that cluster's table: 0 .. 4 * E - 1 its own faces, then E / 2 from the partition before, E / 2 from the one after, 32 of the first and 32 of the second buffer; each of the last E + 64 columns is named by exactly one face. `halo_faces`: within a partition's block, the fine segment names faces below 256, the middle below 512, the coarse below 1024. `interface_send`: entries name faces of the sending cluster: for side 0 the fine, fine, middle cluster of pairs 0, 1, 2; for side 1 the middle, coarse, coarse cluster; each below 4 times that cluster's element count.
All inputs are finite; a program needn't handle non-finite values.
Results may differ from the reference program's by a relative error of at most 0.0003.
Values sent between devices are 32-bit elements; how exact they have to be, the bound alone decides.
A program may use at most 128 MiB of HBM per device.

```python
import math
import jax
import jax.numpy as jnp
import numpy as np
from jax import lax

FIELDS = 9
NODES = 35
FACE_NODES = 15
EF = 64
EM = 128
EC = 256
XP = 8
ELEMS = 344064
N_DOM = 192
N_SUB = 4


def cluster_links(key, elem_count, extra_cols):
    face_total = 4 * elem_count
    shuffle = jax.random.permutation(key, face_total)
    random_cols = jax.random.randint(jax.random.fold_in(key, 1), (face_total,), 0, face_total)
    position = jnp.arange(face_total)
    chosen = jnp.where(position < extra_cols, face_total + position, random_cols).astype(jnp.int32)
    return jnp.zeros((face_total,), jnp.int32).at[shuffle].set(chosen).reshape(4, elem_count)


def send_rows(key, shape, elem_count):
    values = jax.random.randint(key, shape, 0, 4 * elem_count).astype(jnp.int32)
    return values.at[..., 0].set(4 * elem_count - 1)


def draw_neighbour(key, part):
    parts_total = N_DOM * N_SUB
    width_x = XP * N_SUB

    def per_device(device_key):
        return jnp.concatenate([cluster_links(jax.random.fold_in(device_key, 11), EF, EF + 2 * width_x), cluster_links(jax.random.fold_in(device_key, 12), EM, EM + 2 * width_x), cluster_links(jax.random.fold_in(device_key, 13), EC, EC + 2 * width_x)], axis=1)
    blocks = jax.vmap(per_device)(jax.random.split(key, parts_total))
    return jnp.transpose(blocks, (1, 0, 2)).reshape(4, parts_total * (EF + EM + EC))


def draw_halo_faces(key, part):
    parts_total = N_DOM * N_SUB

    def per_device(device_key):
        return jnp.concatenate([send_rows(jax.random.fold_in(device_key, 21), (2, EF // 2), EF), send_rows(jax.random.fold_in(device_key, 22), (2, EM // 2), EM), send_rows(jax.random.fold_in(device_key, 23), (2, EC // 2), EC)], axis=1)
    blocks = jax.vmap(per_device)(jax.random.split(jax.random.fold_in(key, 5), parts_total))
    return jnp.transpose(blocks, (1, 0, 2)).reshape(2, parts_total * ((EF + EM + EC) // 2))


def draw_interface_send(key, part):
    parts_total = N_DOM * N_SUB
    width_x = XP * N_SUB
    senders = ((EF, EF, EM), (EM, EC, EC))

    def per_device(device_key):
        return jnp.stack([jnp.stack([send_rows(jax.random.fold_in(device_key, 10 * side_id + pair_id), (width_x,), senders[side_id][pair_id]) for pair_id in range(3)]) for side_id in range(2)])
    blocks = jax.vmap(per_device)(jax.random.split(jax.random.fold_in(key, 7), parts_total))
    return jnp.transpose(blocks, (1, 2, 0, 3)).reshape(2, 3, parts_total * width_x)


def plant(result, stream_key, low, high):
    longest = result.shape.index(max(result.shape))
    spots = []
    for shift in (0, 1):
        where = [jax.random.randint(jax.random.fold_in(stream_key, axis), (), 0, length) for axis, length in enumerate(result.shape)]
        where[longest] = (where[longest] + shift) % result.shape[longest]
        spots.append(tuple(where))
    return result.at[spots[0]].set(low).at[spots[1]].set(high)


def block_levels(own_key, extent, cuts, smallest, largest):
    def one(dim, shards_of):
        steps = jax.random.uniform(jax.random.fold_in(jax.random.fold_in(own_key, 6), dim), (shards_of,), jnp.float32, smallest / len(cuts), largest / len(cuts))
        return jnp.repeat(jnp.exp(steps), extent[dim] // shards_of).reshape((-1,) + (1,) * (len(extent) - dim - 1))

    gain = one(*cuts[0])
    for cut in cuts[1:]:
        gain = gain * one(*cut)
    return gain


def bell_draw(stream_key, dims, deviation, most, cuts=(), dtype=jnp.bfloat16):
    drawn = deviation * jax.random.normal(stream_key, dims, jnp.float32)
    if cuts:
        drawn = drawn * block_levels(stream_key, dims, cuts, -0.22, 0.18)
    return jnp.clip(drawn, -most, most).astype(dtype)


def setup_inputs(seed: int = 0) -> dict:
    key_list = jax.random.split(jax.random.key(seed), 11)
    return {
        "wavefield": bell_draw(key_list[0], (FIELDS, NODES, ELEMS), 1.0, 6.0, ((2, 768),), jnp.float32),
        "material": jnp.clip(jnp.exp(math.log(4.0) - 2.0794415 * jax.random.uniform(key_list[1], (3, ELEMS), jnp.float32) ** block_levels(key_list[1], (3, ELEMS), ((1, 768),), -0.2, 0.2)), 0.5, 4.0),
        "geometry": bell_draw(key_list[2], (3, 3, ELEMS), 1.0, 4.0, ((2, 768),), jnp.float32),
        "face_scale": jnp.clip(jnp.exp(math.log(2.0) - 1.3862944 * jax.random.uniform(key_list[3], (4, ELEMS), jnp.float32) ** block_levels(key_list[3], (4, ELEMS), ((1, 768),), -0.2, 0.2)), 0.5, 2.0),
        "derivative": bell_draw(key_list[4], (3, NODES, NODES), NODES ** -0.5, 1.0, (), jnp.float32),
        "lift_matrix": bell_draw(key_list[5], (NODES, 4 * FACE_NODES), (4 * FACE_NODES) ** -0.5, 0.75, (), jnp.float32),
        "neighbour": draw_neighbour(jax.random.fold_in(key_list[10], 71), 0),
        "orient": plant(jax.random.randint(key_list[7], (4, ELEMS), 0, 3), jax.random.fold_in(key_list[7], 1), 0, 2).astype(jnp.int32),
        "halo_faces": draw_halo_faces(jax.random.fold_in(key_list[10], 71), 0),
        "interface_send": draw_interface_send(jax.random.fold_in(key_list[10], 71), 0),
    }


PENALTY = 0.5
COARSE_STEP = 0.1
highest = lax.Precision.HIGHEST


def face_tables():
    lattice = [(corner_a, corner_b, corner_c, 4 - corner_a - corner_b - corner_c) for corner_a in range(5) for corner_b in range(5 - corner_a) for corner_c in range(5 - corner_a - corner_b)]
    face_rows = np.array([[number for number, coords in enumerate(lattice) if coords[face_id] == 0] for face_id in range(4)], np.int32)
    triangle = [coords[1:] for coords in lattice if coords[0] == 0]
    position = {coords: number for number, coords in enumerate(triangle)}

    def turned(coords, times_turn):
        flipped = (coords[1], coords[0], coords[2])
        for repeat in range(times_turn):
            flipped = (flipped[1], flipped[2], flipped[0])
        return flipped

    orders = np.array([[position[turned(coords, times_turn)] for coords in triangle] for times_turn in range(3)], np.int32)
    return face_rows, orders


def face_traces(element_state, face_rows):
    elem_count = element_state.shape[2]
    picked = element_state[:, face_rows.reshape(-1), :].reshape(9, 4, 15, elem_count)
    return picked.transpose(0, 2, 1, 3).reshape(135, 4 * elem_count)


def element_rate(element_state, material, geometry, face_scale, trace_table, neighbour, orient, derivative, lift_matrix, face_rows, orders):
    elem_count = element_state.shape[2]
    along_ref = jnp.einsum("kmn,qne->kqme", derivative, element_state, precision=highest)
    physical = jnp.einsum("ike,kqme->iqme", geometry, along_ref, precision=highest)
    density = material[0]
    lame_first = material[1]
    shear_mod = material[2]
    voigt_index = ((3, 8, 7), (8, 4, 6), (7, 6, 5))
    rate_list = []
    for direction in range(3):
        rate_list.append((physical[0, voigt_index[direction][0]] + physical[1, voigt_index[direction][1]] + physical[2, voigt_index[direction][2]]) / density)
    divergence = physical[0, 0] + physical[1, 1] + physical[2, 2]
    for direction in range(3):
        rate_list.append(lame_first * divergence + 2.0 * shear_mod * physical[direction, direction])
    rate_list.append(shear_mod * (physical[1, 2] + physical[2, 1]))
    rate_list.append(shear_mod * (physical[0, 2] + physical[2, 0]))
    rate_list.append(shear_mod * (physical[0, 1] + physical[1, 0]))
    volume = jnp.stack(rate_list)
    own_side = face_traces(element_state, face_rows).reshape(9, 15, 4 * elem_count)
    columns = trace_table.shape[1]
    flat_table = trace_table.reshape(9, 15 * columns)
    node_order = jnp.take(jnp.asarray(orders), orient.reshape(-1), axis=0).transpose(1, 0)
    flat_index = (node_order * columns + neighbour.reshape(-1)[None, :]).astype(jnp.int32)
    aligned = jnp.take(flat_table, flat_index.reshape(-1), axis=1).reshape(9, 15, 4 * elem_count)
    face_jump = (aligned - own_side) * (PENALTY * face_scale.reshape(-1))
    face_jump = face_jump.reshape(9, 15, 4, elem_count).transpose(0, 2, 1, 3).reshape(9, 60, elem_count)
    surface = jnp.einsum("mn,qne->qme", lift_matrix, face_jump, precision=highest)
    return volume + surface


def reference(wavefield, material, geometry, face_scale, derivative, lift_matrix, neighbour, orient, halo_faces, interface_send):
    devices = N_DOM * N_SUB
    per_dev = EF + EM + EC
    width_x = XP * N_SUB
    halo_dev = per_dev // 2
    face_rows, orders = face_tables()

    def by_cluster(array):
        lead_dims = array.shape[:-1]
        moved = jnp.moveaxis(array.reshape(lead_dims + (devices, per_dev)), -2, 0)
        return moved[..., :EF], moved[..., EF:EF + EM], moved[..., EF + EM:]

    states = by_cluster(wavefield)
    mats = by_cluster(material)
    geos = by_cluster(geometry)
    scales = by_cluster(face_scale)
    links = by_cluster(neighbour)
    turns = by_cluster(orient)
    params = [(mats[cluster], geos[cluster], scales[cluster], links[cluster], turns[cluster]) for cluster in range(3)]
    halo_lists = jnp.moveaxis(halo_faces.reshape(2, devices, halo_dev), 1, 0)
    iface_lists = jnp.moveaxis(interface_send.reshape(2, 3, devices, width_x), 2, 0)
    bounds = ((0, EF // 2), (EF // 2, EF // 2 + EM // 2), (EF // 2 + EM // 2, halo_dev))

    def pick(traces, columns):
        index = jnp.broadcast_to(columns[:, None, :], (columns.shape[0], 135, columns.shape[1]))
        return jnp.take_along_axis(traces, index, axis=2)

    def all_traces(field_block):
        return jax.vmap(lambda single: face_traces(single, face_rows))(field_block)

    def group_swap(buffer):
        blocks = buffer.reshape(N_DOM, N_SUB, 135, N_SUB, XP).transpose(0, 3, 2, 1, 4)
        return blocks.reshape(devices, 135, width_x)

    def update(field_block, cluster, own_side, extras, step_size):
        start_col, stop_col = bounds[cluster]
        send = jnp.stack([pick(own_side, halo_lists[:, 0, start_col:stop_col]), pick(own_side, halo_lists[:, 1, start_col:stop_col])], axis=1)
        nothing = jnp.zeros_like(send[:1, 0])
        from_below = jnp.concatenate([nothing, send[:-1, 1]], axis=0)
        from_above = jnp.concatenate([send[1:, 0], nothing], axis=0)
        trace_table = jnp.concatenate([own_side, from_below, from_above] + extras, axis=2)
        mat_c, geo_c, scale_c, link_c, turn_c = params[cluster]

        def per_device(inputs):
            return element_rate(inputs[0], inputs[1], inputs[2], inputs[3], inputs[4], inputs[5], inputs[6], derivative, lift_matrix, face_rows, orders)

        tendency = lax.map(per_device, (field_block, mat_c, geo_c, scale_c, trace_table, link_c, turn_c))
        return field_block + step_size * tendency

    fast_state, mid_state, slow_state = states
    start_mid = all_traces(mid_state)
    start_slow = all_traces(slow_state)
    from_mid_fm = group_swap(pick(start_mid, iface_lists[:, 1, 0]))
    from_slow_fc = group_swap(pick(start_slow, iface_lists[:, 1, 1]))
    from_slow_mc = group_swap(pick(start_slow, iface_lists[:, 1, 2]))
    zero_buffer = jnp.zeros((devices, 135, width_x), jnp.float32)
    halves = [zero_buffer, zero_buffer]
    whole_fc = zero_buffer
    for substep in range(4):
        own_side = all_traces(fast_state)
        halves[substep // 2] = halves[substep // 2] + 0.5 * pick(own_side, iface_lists[:, 0, 0])
        whole_fc = whole_fc + 0.25 * pick(own_side, iface_lists[:, 0, 1])
        fast_state = update(fast_state, 0, own_side, [from_mid_fm, from_slow_fc], COARSE_STEP / 4)
    recv_first = group_swap(halves[0])
    recv_second = group_swap(halves[1])
    recv_fc = group_swap(whole_fc)
    mid_sum = zero_buffer
    for substep in range(2):
        own_side = start_mid if substep == 0 else all_traces(mid_state)
        mid_sum = mid_sum + 0.5 * pick(own_side, iface_lists[:, 0, 2])
        mid_state = update(mid_state, 1, own_side, [(recv_first, recv_second)[substep], from_slow_mc], COARSE_STEP / 2)
    recv_mc = group_swap(mid_sum)
    slow_state = update(slow_state, 2, start_slow, [recv_fc, recv_mc], COARSE_STEP)
    joined = jnp.concatenate([fast_state, mid_state, slow_state], axis=-1)
    return jnp.moveaxis(joined, 0, 2).reshape(9, 35, devices * per_dev)
```

```python
import functools

import jax
import jax.numpy as jnp
import numpy as np
from jax import lax
from jax.experimental import pallas as pl
from jax.experimental.pallas import tpu as pltpu
from jax.sharding import PartitionSpec as P

F32 = jnp.float32
BF16 = jnp.bfloat16
MESH = pl.DeviceIdType.MESH
N_SUB = 4
COARSE_STEP = 0.1

LANE = (0, 64, 192)
WIDE = (128, 128, 256)
OWN = (512, 512, 1024)
EXT = (128, 256, 384)
SENT = (128, 256, 384)
STEP = (COARSE_STEP / 4, COARSE_STEP / 2, COARSE_STEP)

VOIGT = ((3, 8, 7), (8, 4, 6), (7, 6, 5))


def face_tables():
    lattice = [
        (a, b, c, 4 - a - b - c) for a in range(5) for b in range(5 - a) for c in range(5 - a - b)
    ]
    face_rows = np.array(
        [[i for i, p in enumerate(lattice) if p[f] == 0] for f in range(4)], np.int32
    )
    triangle = [p[1:] for p in lattice if p[0] == 0]
    position = {p: i for i, p in enumerate(triangle)}

    def turned(p, times):
        p = (p[1], p[0], p[2])
        for _ in range(times):
            p = (p[1], p[2], p[0])
        return p

    orders = np.array(
        [[position[turned(p, o)] for p in triangle] for o in range(3)], np.int32
    )
    return face_rows, orders


def constants():
    face_rows, orders = face_tables()
    place = np.zeros((2, 128, 144), np.float32)
    for n in range(35):
        place[0, n, n] = 1
        place[0, n, 48 + n] = 1
        place[1, n, 96 + n] = 1
    select = np.zeros((128, 144), np.float32)
    for f in range(4):
        for n in range(15):
            select[f * 16 + n, face_rows[f, n]] = 1
            select[64 + f * 16 + n, 48 + face_rows[f, n]] = 1
    spread = np.zeros((128, 256), np.float32)
    for f in range(4):
        for n in range(15):
            for o in range(3):
                spread[f * 15 + n, (o * 4 + f) * 16 + orders[o, n]] = 1
            spread[f * 15 + n, 192 + f * 16 + n] = -1
    return place, select, spread


def split(x):
    high = x.astype(BF16)
    return high, (x - high.astype(F32)).astype(BF16)


def dot(a, b):
    return jnp.dot(a, b, preferred_element_type=F32)


def lanes(shape):
    return lax.broadcasted_iota(jnp.int32, shape, 1)


def turn(x, shift):
    shift %= 128
    return pltpu.roll(x, shift, 1) if shift else x


def one_hot(rows, base, index):
    iota = lax.broadcasted_iota(jnp.int32, (rows, index.shape[1]), 0)
    hit = iota == jnp.broadcast_to(index - base, iota.shape)
    return jnp.where(hit, 1.0, 0.0).astype(BF16)


def kernel(
    n_dom,
    wave, mat, geo, fs, der, lift, nbr, ori, halo, iface, place, select, spread,
    out,
    u0, u1, u2, v0, v1, v2, t0, t1, t2, g0, g1, g2, stack, prod, jump,
    oh0, oh1, oh2, os0, os1, os2, cf0, cf1, cf2, sc0, sc1, sc2, om0, om1, om2,
    dpad, lpad, amat, lmat, sent0, sent1, sent2, sum_a, sum_b, base0,
    hs0, hr0, hs1, hr1, hs2, hr2, gs0, gr0, gs1, gr1, gs2, gr2, gs3, gr3,
    ss0, rs0, ss1, rs1, ss2, rs2, gss, grs,
):
    us, vs, ts, gs_, ohs, oss = (u0, u1, u2), (v0, v1, v2), (t0, t1, t2), (g0, g1, g2), (oh0, oh1, oh2), (os0, os1, os2)
    cfs, scs, oms, sents = (cf0, cf1, cf2), (sc0, sc1, sc2), (om0, om1, om2), (sent0, sent1, sent2)
    total = n_dom * N_SUB
    dom = lax.axis_index("dom")
    sub = lax.axis_index("sub")
    me = dom * N_SUB + sub
    up = (me + 1) % total
    down = (me + total - 1) % total
    up_id = (up // N_SUB, up % N_SUB)
    down_id = (down // N_SUB, down % N_SUB)
    not_first = jnp.where(me == 0, 0.0, 1.0).astype(F32)
    not_last = jnp.where(me == total - 1, 0.0, 1.0).astype(F32)

    barrier = pltpu.get_barrier_semaphore()
    pl.semaphore_signal(barrier, inc=1, device_id=up_id, device_id_type=MESH)
    pl.semaphore_signal(barrier, inc=1, device_id=down_id, device_id_type=MESH)
    for k in range(1, N_SUB):
        pl.semaphore_signal(
            barrier, inc=1, device_id=(dom, (sub + k) % N_SUB), device_id_type=MESH
        )

    def halo_copies(send, recv, ssem, rsem, slot):
        return [
            pltpu.make_async_remote_copy(
                src_ref=send.at[slot, way], dst_ref=recv.at[slot, way],
                send_sem=ssem.at[slot, way], recv_sem=rsem.at[slot, way],
                device_id=(up_id, down_id)[way], device_id_type=MESH,
            )
            for way in range(2)
        ]

    def group_copies(send, recv, number):
        found = []
        for k in range(1, N_SUB):
            dest = (sub + k) % N_SUB
            found.append(
                pltpu.make_async_remote_copy(
                    src_ref=send.at[dest], dst_ref=recv.at[sub],
                    send_sem=gss.at[number, k], recv_sem=grs.at[number, k],
                    device_id=(dom, dest), device_id_type=MESH,
                )
            )
        return found

    halo_f = [halo_copies(hs0, hr0, ss0, rs0, s) for s in range(4)]
    halo_m = [halo_copies(hs1, hr1, ss1, rs1, s) for s in range(2)]
    halo_c = halo_copies(hs2, hr2, ss2, rs2, 0)
    group = [
        group_copies(s, r, i)
        for i, (s, r) in enumerate(((gs0, gr0), (gs1, gr1), (gs2, gr2), (gs3, gr3)))
    ]

    dpad[...] = jnp.zeros_like(dpad)
    lpad[...] = jnp.zeros_like(lpad)
    for k in range(3):
        dpad[k, 0:35, 0:35] = der[k]
    lpad[0:35, 0:60] = lift[...]
    parts = []
    for k in range(3):
        high, low = split(dpad[k])
        parts.append(dot(high, place[0]) + dot(low, place[1]))
    amat[...] = jnp.concatenate(parts + [select[...]], axis=0).astype(BF16)
    high, low = split(lpad[...])
    lmat[0:48] = dot(high, spread[...]).astype(BF16)
    lmat[48:96] = dot(low, spread[...]).astype(BF16)

    def remap(index, c):
        if c:
            return index
        return jnp.where(
            index < 256, (index & 63) + ((index >> 6) << 7), index + 256
        )

    def load(c):
        first, wide = LANE[c], WIDE[c]
        span = slice(first, first + wide)
        u = us[c]
        for q in range(9):
            u[q, 32:40, :] = jnp.zeros((8, wide), F32)
            u[q, 0:35, :] = wave[q, :, span]
        rho = STEP[c] / mat[0:1, span]
        lam = STEP[c] * mat[1:2, span]
        mu = STEP[c] * mat[2:3, span]
        cf = cfs[c]
        for i in range(3):
            axes = geo[i, :, span]
            cf[3 * i : 3 * i + 3] = axes * mu
            cf[9 + 3 * i : 12 + 3 * i] = axes * rho
            cf[18 + 3 * i : 21 + 3 * i] = axes
        cf[27:28] = lam
        cf[28:29] = 2.0 * mu
        for f in range(4):
            where = slice(f * wide, (f + 1) * wide)
            scs[c][:, where] = (0.5 * STEP[c]) * fs[f : f + 1, span]
            row = jnp.broadcast_to(ori[f : f + 1, span], (16, wide))
            for o in range(3):
                oms[c][o, :, where] = jnp.where(row == o, 1.0, 0.0).astype(BF16)

    def send_tables():
        low, high = halo[0:1, 0:32], halo[1:2, 0:32]
        row = jnp.concatenate([low, high, iface[0, 0:1], iface[0, 1:2]], axis=1)
        os0[...] = one_hot(512, 0, remap(row, 0))
        row = jnp.concatenate([halo[0:1, 32:96], halo[1:2, 32:96]], axis=1)
        os1[:, 0:128] = one_hot(512, 0, row)
        blank = jnp.full((1, 64), -1, jnp.int32)
        row = jnp.concatenate([iface[1, 0:1], iface[0, 2:3], blank], axis=1)
        os1[:, 128:256] = one_hot(512, 0, row)
        os2[:, 0:128] = one_hot(1024, 0, halo[0:1, 96:224])
        os2[:, 128:256] = one_hot(1024, 0, halo[1:2, 96:224])
        row = jnp.concatenate([iface[1, 1:2], iface[1, 2:3], blank], axis=1)
        os2[:, 256:384] = one_hot(1024, 0, row)

    def neighbour_table(c):
        span = slice(LANE[c], LANE[c] + WIDE[c])
        for f in range(4):
            where = slice(f * WIDE[c], (f + 1) * WIDE[c])
            index = remap(nbr[f : f + 1, span], c)
            ohs[c][:, where] = one_hot(OWN[c] + EXT[c], 0, index)

    def traces(c):
        wide = WIDE[c]
        u, t = us[c], ts[c]
        gap = jnp.zeros((8, wide), F32)
        for q in range(9):
            x = u[q]
            high = x.astype(BF16).astype(F32)
            tall = jnp.concatenate([high, gap, x - high, gap, high, gap], axis=0)
            stack[:, q * wide : (q + 1) * wide] = tall.astype(BF16)
        span = 9 * wide
        prod[:, 0:span] = dot(amat[...], stack[:, 0:span])
        for q in range(9):
            where = slice(q * wide, (q + 1) * wide)
            for part in range(2):
                for f in range(4):
                    row = 120 + 64 * part + 16 * f
                    t[144 * part + 16 * q : 144 * part + 16 * q + 16, f * wide : (f + 1) * wide] = (
                        prod[row : row + 16, where].astype(BF16)
                    )
        both = dot(t[:, 0 : OWN[c]], oss[c][...])
        sents[c][...] = both[0:144] + both[144:288]

    def volume(c):
        wide = WIDE[c]
        cf = cfs[c]
        for start in range(0, wide, 128):
            span = slice(start, start + 128)

            def grad(q, i, kind):
                at = q * wide + start
                base = 9 * kind + 3 * i
                return sum(
                    jnp.broadcast_to(cf[base + k : base + k + 1, span], (40, 128))
                    * prod[40 * k : 40 * k + 40, at : at + 128]
                    for k in range(3)
                )

            for i in range(3):
                rate = grad(VOIGT[i][0], 0, 1) + grad(VOIGT[i][1], 1, 1) + grad(VOIGT[i][2], 2, 1)
                vs[c][i, :, span] = us[c][i, :, span] + rate
            diag = [grad(i, i, 2) for i in range(3)]
            shared = cf[27:28, span] * (diag[0] + diag[1] + diag[2])
            for i in range(3):
                vs[c][3 + i, :, span] = us[c][3 + i, :, span] + (shared + cf[28:29, span] * diag[i])
            for q, i, j in ((6, 1, 2), (7, 0, 2), (8, 0, 1)):
                rate = grad(j, i, 0) + grad(i, j, 0)
                vs[c][q, :, span] = us[c][q, :, span] + rate
        both = dot(ts[c][:, 0 : OWN[c]], ohs[c][0 : OWN[c]])
        gs_[c][...] = both[0:144] + both[144:288]

    def store_ext(c, at, value):
        high, low = split(value)
        ts[c][0:144, OWN[c] + at : OWN[c] + at + 128] = high
        ts[c][144:288, OWN[c] + at : OWN[c] + at + 128] = low

    def finish(c):
        wide, own = WIDE[c], OWN[c]
        t = ts[c]
        both = dot(t[:, own:], ohs[c][own:])
        gs_[c][...] += both[0:144] + both[144:288]
        scale = scs[c][...]
        for q in range(9):
            rows = slice(16 * q, 16 * q + 16)
            low_rows = slice(144 + 16 * q, 160 + 16 * q)
            high, low = split(gs_[c][rows] * scale)
            mine = t[rows, 0:own].astype(F32) + t[low_rows, 0:own].astype(F32)
            own_high, own_low = split(mine * scale)
            where = slice(q * wide, (q + 1) * wide)
            for f in range(4):
                face = slice(f * wide, (f + 1) * wide)
                for o in range(3):
                    mask = oms[c][o, :, face]
                    at = (4 * o + f) * 16
                    jump[0, at : at + 16, where] = high[:, face] * mask
                    jump[1, at : at + 16, where] = low[:, face] * mask
                at = 192 + 16 * f
                jump[0, at : at + 16, where] = own_high[:, face]
                jump[1, at : at + 16, where] = own_low[:, face]
        span = 9 * wide
        first = dot(lmat[...], jump[0, :, 0:span])
        second = dot(lmat[0:48], jump[1, :, 0:span])
        whole = first[0:40] + first[48:88] + second[0:40]
        for q in range(9):
            us[c][q] = vs[c][q] + whole[:, q * wide : (q + 1) * wide]

    lane48 = lanes((48, 128))
    lane16 = lanes((16, 128))

    def pack_third(x, base):
        return jnp.where(
            lane48 < 32, turn(x[0:48], -base),
            jnp.where(lane48 < 64, turn(x[48:96], 32 - base), turn(x[96:144], 64 - base)),
        )

    def send_fine(slot):
        x = sent0[...]
        hs0[slot, 0] = pack_third(x, 32)
        hs0[slot, 1] = pack_third(x, 0)

    def send_middle(slot):
        x = sent1[:, 0:128]
        lower = x[0:80]
        upper = jnp.concatenate([x[80:144], jnp.zeros((16, 128), F32)], axis=0)
        left = lanes((80, 128)) < 64
        hs1[slot, 0] = jnp.where(left, turn(lower, 64), upper)
        hs1[slot, 1] = jnp.where(left, lower, turn(upper, 64))

    def send_group(send, recv, number, x, base):
        rows = slice(16 * number, 16 * number + 16)
        for j in range(N_SUB):
            acc = jnp.zeros((16, 128), F32)
            for q in range(9):
                piece = turn(x[16 * q : 16 * q + 16], 8 * q - base - 8 * j)
                acc = jnp.where((lane16 >= 8 * q) & (lane16 < 8 * q + 8), piece, acc)
            send[j, rows] = acc
        recv[sub, rows] = send[sub, rows]

    def take_group(recv, number, base):
        rows = slice(16 * number, 16 * number + 16)
        pieces = [recv[p, rows] for p in range(N_SUB)]
        found = []
        for q in range(9):
            acc = jnp.zeros((16, 128), F32)
            for p in range(N_SUB):
                at = base + 8 * p
                acc = jnp.where(
                    (lane16 >= at) & (lane16 < at + 8), turn(pieces[p], at - 8 * q), acc
                )
            found.append(acc)
        return jnp.concatenate(found, axis=0)

    def start(copies):
        for copy in copies:
            copy.start()

    def arrive(copies):
        for copy in copies:
            copy.wait_recv()

    def fine_ext(slot):
        below = hr0[slot, 0] * not_first
        above = hr0[slot, 1] * not_last
        found = []
        for r in range(3):
            found.append(
                jnp.where(
                    lane48 < 32, turn(below, -32 * r),
                    jnp.where(lane48 < 64, turn(above, 32 - 32 * r), base0[48 * r : 48 * r + 48]),
                )
            )
        store_ext(0, 0, jnp.concatenate(found, axis=0))

    def middle_ext(slot):
        below = hr1[slot, 0] * not_first
        above = hr1[slot, 1] * not_last
        left = lanes((80, 128)) < 64
        lower = jnp.where(left, below, turn(above, 64))
        upper = jnp.where(left, turn(below, 64), above)
        store_ext(1, 0, jnp.concatenate([lower, upper[0:64]], axis=0))

    load(0)
    send_tables()
    traces(0)
    sum_a[...] = sent0[...]
    send_fine(0)
    pl.semaphore_wait(barrier, 2 + N_SUB - 1)
    start(halo_f[0])
    neighbour_table(0)
    volume(0)
    load(1)
    traces(1)
    send_middle(0)
    start(halo_m[0])
    sum_b[...] = sent1[:, 128:256]
    send_group(gs0, gr0, 0, sent1[:, 128:256], 0)
    neighbour_table(1)
    volume(1)
    load(2)
    traces(2)
    send_group(gs0, gr0, 1, sent2[:, 256:384], 0)
    send_group(gs0, gr0, 2, sent2[:, 256:384], 32)
    start(group[0])
    hs2[0, 0] = sent2[:, 128:256]
    hs2[0, 1] = sent2[:, 0:128]
    start(halo_c)
    neighbour_table(2)
    volume(2)
    arrive(group[0])
    base0[...] = take_group(gr0, 0, 64) + take_group(gr0, 1, 96)
    start_mc = take_group(gr0, 2, 32)

    arrive(halo_f[0])
    fine_ext(0)
    finish(0)
    traces(0)
    send_fine(1)
    start(halo_f[1])
    sum_a[...] += sent0[...]
    send_group(gs1, gr1, 0, 0.5 * sum_a[...], 64)
    start(group[1])
    volume(0)
    arrive(halo_m[0])
    middle_ext(0)

    arrive(halo_f[1])
    fine_ext(1)
    finish(0)
    traces(0)
    send_fine(2)
    start(halo_f[2])
    sum_a[...] = 0.25 * sum_a[...] + 0.25 * sent0[...]
    base1 = sent0[...]
    volume(0)

    arrive(group[1])
    store_ext(1, 128, take_group(gr1, 0, 0) + start_mc)
    finish(1)
    traces(1)
    send_middle(1)
    start(halo_m[1])
    send_group(gs2, gr2, 0, 0.5 * (sum_b[...] + sent1[:, 128:256]), 32)
    start(group[2])
    volume(1)

    arrive(halo_f[2])
    fine_ext(2)
    finish(0)
    traces(0)
    send_fine(3)
    start(halo_f[3])
    sum_a[...] += 0.25 * sent0[...]
    send_group(gs3, gr3, 0, 0.5 * (base1 + sent0[...]), 64)
    send_group(gs3, gr3, 1, sum_a[...], 96)
    start(group[3])
    volume(0)
    arrive(halo_c)
    store_ext(2, 0, hr2[0, 0] * not_first)
    store_ext(2, 128, hr2[0, 1] * not_last)
    arrive(halo_m[1])
    middle_ext(1)

    arrive(halo_f[3])
    fine_ext(3)
    finish(0)
    arrive(group[3])
    store_ext(1, 128, take_group(gr3, 0, 0) + start_mc)
    finish(1)
    arrive(group[2])
    store_ext(2, 256, take_group(gr3, 1, 0) + take_group(gr2, 0, 32))
    finish(2)
    for q in range(9):
        out[q, :, 0:64] = u0[q, 0:35, 0:64]
        out[q, :, 64:192] = u1[q, 0:35, :]
        out[q, :, 192:448] = u2[q, 0:35, :]
    for copies in halo_f + halo_m + [halo_c] + group:
        for copy in copies:
            copy.wait_send()


def scratch():
    shapes = []
    shapes += [pltpu.VMEM((9, 40, w), F32) for w in WIDE] * 2
    shapes += [pltpu.VMEM((288, o + e), BF16) for o, e in zip(OWN, EXT)]
    shapes += [pltpu.VMEM((144, o), F32) for o in OWN]
    shapes += [pltpu.VMEM((144, 9 * 256), BF16), pltpu.VMEM((248, 9 * 256), F32)]
    shapes += [pltpu.VMEM((2, 256, 9 * 256), BF16)]
    shapes += [pltpu.VMEM((o + e, o), BF16) for o, e in zip(OWN, EXT)]
    shapes += [pltpu.VMEM((o, s), BF16) for o, s in zip(OWN, SENT)]
    shapes += [pltpu.VMEM((32, w), F32) for w in WIDE]
    shapes += [pltpu.VMEM((1, o), F32) for o in OWN]
    shapes += [pltpu.VMEM((3, 16, o), BF16) for o in OWN]
    shapes += [pltpu.VMEM((3, 40, 128), F32), pltpu.VMEM((48, 128), F32)]
    shapes += [pltpu.VMEM((248, 144), BF16), pltpu.VMEM((96, 256), BF16)]
    shapes += [pltpu.VMEM((144, s), F32) for s in SENT]
    shapes += [pltpu.VMEM((144, 128), F32)] * 3
    shapes += [pltpu.VMEM((4, 2, 48, 128), F32)] * 2
    shapes += [pltpu.VMEM((2, 2, 80, 128), F32)] * 2
    shapes += [pltpu.VMEM((1, 2, 144, 128), F32)] * 2
    for buffers in (3, 1, 1, 2):
        shapes += [pltpu.VMEM((N_SUB, 16 * buffers, 128), F32)] * 2
    for slots in (4, 2, 1):
        shapes += [pltpu.SemaphoreType.DMA((slots, 2))] * 2
    shapes += [pltpu.SemaphoreType.DMA((4, 4))] * 2
    return shapes


def solution(mesh):
    n_dom = mesh.shape["dom"]
    place, select, spread = constants()

    def on_device(*arrays):
        consts = (
            jnp.asarray(place, BF16), jnp.asarray(select, F32), jnp.asarray(spread, BF16),
        )
        return pl.pallas_call(
            functools.partial(kernel, n_dom),
            out_shape=jax.ShapeDtypeStruct(arrays[0].shape, F32),
            in_specs=[pl.BlockSpec(memory_space=pltpu.VMEM)] * 13,
            out_specs=pl.BlockSpec(memory_space=pltpu.VMEM),
            scratch_shapes=scratch(),
            compiler_params=pltpu.CompilerParams(
                collective_id=0, has_side_effects=True, vmem_limit_bytes=60 * 1024 * 1024
            ),
            name="step",
        )(*arrays, *consts)

    split_all = ("dom", "sub")
    placed = (
        P(None, None, split_all), P(None, split_all), P(None, None, split_all),
        P(None, split_all), P(), P(), P(None, split_all), P(None, split_all),
        P(None, split_all), P(None, None, split_all),
    )
    return jax.shard_map(
        on_device, mesh=mesh, in_specs=placed, out_specs=P(None, None, split_all), check_vma=False,
    )
```

```python
import functools

import jax
import jax.numpy as jnp
import numpy as np
from jax import lax
from jax.experimental import pallas as pl
from jax.experimental.pallas import tpu as pltpu
from jax.sharding import PartitionSpec as P

F32 = jnp.float32
BF16 = jnp.bfloat16
MESH = pl.DeviceIdType.MESH
N_SUB = 4
COARSE_STEP = 0.1

LANE = (0, 64, 192)
WIDE = (128, 128, 256)
OWN = (512, 512, 1024)
EXT = (128, 256, 384)
SENT = (128, 256, 384)
STEP = (COARSE_STEP / 4, COARSE_STEP / 2, COARSE_STEP)

VOIGT = ((3, 8, 7), (8, 4, 6), (7, 6, 5))


def face_tables():
    lattice = [
        (a, b, c, 4 - a - b - c) for a in range(5) for b in range(5 - a) for c in range(5 - a - b)
    ]
    face_rows = np.array(
        [[i for i, p in enumerate(lattice) if p[f] == 0] for f in range(4)], np.int32
    )
    triangle = [p[1:] for p in lattice if p[0] == 0]
    position = {p: i for i, p in enumerate(triangle)}

    def turned(p, times):
        p = (p[1], p[0], p[2])
        for _ in range(times):
            p = (p[1], p[2], p[0])
        return p

    orders = np.array(
        [[position[turned(p, o)] for p in triangle] for o in range(3)], np.int32
    )
    return face_rows, orders


def constants():
    face_rows, orders = face_tables()
    place = np.zeros((2, 128, 144), np.float32)
    for n in range(35):
        place[0, n, n] = 1
        place[0, n, 48 + n] = 1
        place[1, n, 96 + n] = 1
    select = np.zeros((128, 144), np.float32)
    for f in range(4):
        for n in range(15):
            select[f * 16 + n, face_rows[f, n]] = 1
            select[64 + f * 16 + n, 48 + face_rows[f, n]] = 1
    spread = np.zeros((128, 256), np.float32)
    for f in range(4):
        for n in range(15):
            for o in range(3):
                spread[f * 15 + n, (o * 4 + f) * 16 + orders[o, n]] = 1
            spread[f * 15 + n, 192 + f * 16 + n] = -1
    return place, select, spread


def split(x):
    high = x.astype(BF16)
    return high, (x - high.astype(F32)).astype(BF16)


def dot(a, b):
    return jnp.dot(a, b, preferred_element_type=F32)


def lanes(shape):
    return lax.broadcasted_iota(jnp.int32, shape, 1)


def turn(x, shift):
    shift %= 128
    return pltpu.roll(x, shift, 1) if shift else x


def one_hot(rows, base, index):
    iota = lax.broadcasted_iota(jnp.int32, (rows, index.shape[1]), 0)
    hit = iota == jnp.broadcast_to(index - base, iota.shape)
    return jnp.where(hit, 1.0, 0.0).astype(BF16)


def kernel(
    n_dom,
    *refs,
):
    ins, out, held, in_sems, rest = refs[:13], refs[13], refs[14:27], refs[27], refs[28:]
    body(n_dom, ins, in_sems, out, *held, *rest)


def body(
    n_dom, ins, in_sems, out,
    wave, mat, geo, fs, der, lift, nbr, ori, halo, iface, place, select, spread,
    u0, u1, u2, v0, v1, v2, t0, t1, t2, g0, g1, g2, stack, prod0, prod1, prod2, jump,
    oh0, oh1, oh2, os0, os1, os2, cf0, cf1, cf2, sc0, sc1, sc2, om0, om1, om2,
    dpad, lpad, amat, lmat, sent0, sent1, sent2, sum_a, sum_b, base0,
    hs0, hr0, hs1, hr1, hs2, hr2, gs0, gr0, gs1, gr1, gs2, gr2, gs3, gr3,
    ss0, rs0, ss1, rs1, ss2, rs2, gss, grs,
):
    us, vs, ts, gs_, ohs, oss = (u0, u1, u2), (v0, v1, v2), (t0, t1, t2), (g0, g1, g2), (oh0, oh1, oh2), (os0, os1, os2)
    cfs, scs, oms, sents = (cf0, cf1, cf2), (sc0, sc1, sc2), (om0, om1, om2), (sent0, sent1, sent2)
    prods = (prod0, prod1, prod2)
    total = n_dom * N_SUB
    dom = lax.axis_index("dom")
    sub = lax.axis_index("sub")
    me = dom * N_SUB + sub
    up = (me + 1) % total
    down = (me + total - 1) % total
    up_id = (up // N_SUB, up % N_SUB)
    down_id = (down // N_SUB, down % N_SUB)
    first, last = me == 0, me == total - 1

    barrier = pltpu.get_barrier_semaphore()

    @pl.when(jnp.logical_not(last))
    def _():
        pl.semaphore_signal(barrier, inc=1, device_id=up_id, device_id_type=MESH)

    @pl.when(jnp.logical_not(first))
    def _():
        pl.semaphore_signal(barrier, inc=1, device_id=down_id, device_id_type=MESH)

    for k in range(1, N_SUB):
        pl.semaphore_signal(
            barrier, inc=1, device_id=(dom, (sub + k) % N_SUB), device_id_type=MESH
        )

    def halo_copies(send, recv, ssem, rsem, slot):
        return [
            pltpu.make_async_remote_copy(
                src_ref=send.at[slot, way], dst_ref=recv.at[slot, way],
                send_sem=ssem.at[slot, way], recv_sem=rsem.at[slot, way],
                device_id=(up_id, down_id)[way], device_id_type=MESH,
            )
            for way in range(2)
        ]

    def group_copies(send, recv, number):
        found = []
        for k in range(1, N_SUB):
            dest = (sub + k) % N_SUB
            found.append(
                pltpu.make_async_remote_copy(
                    src_ref=send.at[dest], dst_ref=recv.at[sub],
                    send_sem=gss.at[number, k], recv_sem=grs.at[number, k],
                    device_id=(dom, dest), device_id_type=MESH,
                )
            )
        return found

    held = (wave, mat, geo, fs, der, lift, nbr, ori, halo, iface, place, select, spread)
    fetch = {
        i: pltpu.make_async_copy(ins[i], held[i], in_sems.at[i])
        for i in (4, 5, 10, 11, 12, 0, 8, 9, 1, 2, 3, 7, 6)
    }
    for copy in fetch.values():
        copy.start()

    def fetched(*numbers):
        for i in numbers:
            fetch[i].wait()

    for end, way in ((first, 0), (last, 1)):

        @pl.when(end)
        def _():
            for ref in (hr0, hr1, hr2):
                ref[:, way] = jnp.zeros((ref.shape[0],) + ref.shape[2:], F32)

    halo_f = [halo_copies(hs0, hr0, ss0, rs0, s) for s in range(4)]
    halo_m = [halo_copies(hs1, hr1, ss1, rs1, s) for s in range(2)]
    halo_c = halo_copies(hs2, hr2, ss2, rs2, 0)
    group = [
        group_copies(s, r, i)
        for i, (s, r) in enumerate(((gs0, gr0), (gs1, gr1), (gs2, gr2), (gs3, gr3)))
    ]

    dpad[...] = jnp.zeros_like(dpad)
    lpad[...] = jnp.zeros_like(lpad)
    fetched(4, 5, 10, 11, 12)
    for k in range(3):
        dpad[k, 0:35, 0:35] = der[k]
    lpad[0:35, 0:60] = lift[...]
    parts = []
    for k in range(3):
        high, low = split(dpad[k])
        parts.append(dot(high, place[0]) + dot(low, place[1]))
    amat[...] = jnp.concatenate(parts + [select[...]], axis=0).astype(BF16)
    high, low = split(lpad[...])
    lmat[0:48] = dot(high, spread[...]).astype(BF16)
    lmat[48:96] = dot(low, spread[...]).astype(BF16)

    def remap(index, c):
        if c:
            return index
        return jnp.where(
            index < 256, (index & 63) + ((index >> 6) << 7), index + 256
        )

    def load(c):
        first, wide = LANE[c], WIDE[c]
        span = slice(first, first + wide)
        u = us[c]
        for q in range(9):
            u[q, 32:40, :] = jnp.zeros((8, wide), F32)
            u[q, 0:35, :] = wave[q, :, span]

    def coefficients(c):
        first, wide = LANE[c], WIDE[c]
        span = slice(first, first + wide)
        rho = STEP[c] / mat[0:1, span]
        lam = STEP[c] * mat[1:2, span]
        mu = STEP[c] * mat[2:3, span]
        cf = cfs[c]
        for i in range(3):
            axes = geo[i, :, span]
            cf[3 * i : 3 * i + 3] = axes * mu
            cf[9 + 3 * i : 12 + 3 * i] = axes * rho
            cf[18 + 3 * i : 21 + 3 * i] = axes
        cf[27:28] = lam
        cf[28:29] = 2.0 * mu
        for f in range(4):
            where = slice(f * wide, (f + 1) * wide)
            scs[c][:, where] = (0.5 * STEP[c]) * fs[f : f + 1, span]
            row = jnp.broadcast_to(ori[f : f + 1, span], (16, wide))
            for o in range(3):
                oms[c][o, :, where] = jnp.where(row == o, 1.0, 0.0).astype(BF16)

    def send_table(c):
        blank = jnp.full((1, 64), -1, jnp.int32)
        if c == 0:
            rows = [(halo[0:1, 0:32], halo[1:2, 0:32], iface[0, 0:1], iface[1, 0:1])]
        elif c == 1:
            rows = [(halo[0:1, 32:96], halo[1:2, 32:96]), (iface[0, 1:2], iface[2, 0:1], blank)]
        else:
            rows = [
                (halo[0:1, 96:224],), (halo[1:2, 96:224],), (iface[1, 1:2], iface[2, 1:2], blank),
            ]
        for i, row in enumerate(rows):
            index = remap(jnp.concatenate(row, axis=1), c)
            oss[c][:, 128 * i : 128 * i + 128] = one_hot(OWN[c], 0, index)

    def neighbour_table(c):
        span = slice(LANE[c], LANE[c] + WIDE[c])
        for f in range(4):
            where = slice(f * WIDE[c], (f + 1) * WIDE[c])
            index = remap(nbr[f : f + 1, span], c)
            ohs[c][:, where] = one_hot(OWN[c] + EXT[c], 0, index)

    def traces(c):
        wide = WIDE[c]
        u, t, prod = us[c], ts[c], prods[c]
        gap = jnp.zeros((8, wide), F32)
        for q in range(9):
            x = u[q]
            high = x.astype(BF16).astype(F32)
            tall = jnp.concatenate([high, gap, x - high, gap, high, gap], axis=0)
            stack[:, q * wide : (q + 1) * wide] = tall.astype(BF16)
        span = 9 * wide
        prod[...] = dot(amat[...], stack[:, 0:span])
        for q in range(9):
            where = slice(q * wide, (q + 1) * wide)
            for part in range(2):
                for f in range(4):
                    row = 120 + 64 * part + 16 * f
                    t[144 * part + 16 * q : 144 * part + 16 * q + 16, f * wide : (f + 1) * wide] = (
                        prod[row : row + 16, where].astype(BF16)
                    )
        both = dot(t[:, 0 : OWN[c]], oss[c][...])
        sents[c][...] = both[0:144] + both[144:288]

    def volume(c):
        wide = WIDE[c]
        cf, prod = cfs[c], prods[c]
        for start in range(0, wide, 128):
            span = slice(start, start + 128)

            def grad(q, i, kind):
                at = q * wide + start
                base = 9 * kind + 3 * i
                return sum(
                    jnp.broadcast_to(cf[base + k : base + k + 1, span], (40, 128))
                    * prod[40 * k : 40 * k + 40, at : at + 128]
                    for k in range(3)
                )

            for i in range(3):
                rate = grad(VOIGT[i][0], 0, 1) + grad(VOIGT[i][1], 1, 1) + grad(VOIGT[i][2], 2, 1)
                vs[c][i, :, span] = us[c][i, :, span] + rate
            diag = [grad(i, i, 2) for i in range(3)]
            shared = cf[27:28, span] * (diag[0] + diag[1] + diag[2])
            for i in range(3):
                vs[c][3 + i, :, span] = us[c][3 + i, :, span] + (shared + cf[28:29, span] * diag[i])
            for q, i, j in ((6, 1, 2), (7, 0, 2), (8, 0, 1)):
                rate = grad(j, i, 0) + grad(i, j, 0)
                vs[c][q, :, span] = us[c][q, :, span] + rate
        both = dot(ts[c][:, 0 : OWN[c]], ohs[c][0 : OWN[c]])
        gs_[c][...] = both[0:144] + both[144:288]

    def store_ext(c, at, value):
        high, low = split(value)
        ts[c][0:144, OWN[c] + at : OWN[c] + at + 128] = high
        ts[c][144:288, OWN[c] + at : OWN[c] + at + 128] = low

    def finish(c):
        wide, own = WIDE[c], OWN[c]
        t = ts[c]
        both = dot(t[:, own:], ohs[c][own:])
        gs_[c][...] += both[0:144] + both[144:288]
        scale = scs[c][...]
        for q in range(9):
            rows = slice(16 * q, 16 * q + 16)
            low_rows = slice(144 + 16 * q, 160 + 16 * q)
            high, low = split(gs_[c][rows] * scale)
            mine = t[rows, 0:own].astype(F32) + t[low_rows, 0:own].astype(F32)
            own_high, own_low = split(mine * scale)
            where = slice(q * wide, (q + 1) * wide)
            for f in range(4):
                face = slice(f * wide, (f + 1) * wide)
                for o in range(3):
                    mask = oms[c][o, :, face]
                    at = (4 * o + f) * 16
                    jump[0, at : at + 16, where] = high[:, face] * mask
                    jump[1, at : at + 16, where] = low[:, face] * mask
                at = 192 + 16 * f
                jump[0, at : at + 16, where] = own_high[:, face]
                jump[1, at : at + 16, where] = own_low[:, face]
        span = 9 * wide
        first = dot(lmat[...], jump[0, :, 0:span])
        second = dot(lmat[0:48], jump[1, :, 0:span])
        whole = first[0:40] + first[48:88] + second[0:40]
        for q in range(9):
            us[c][q] = vs[c][q] + whole[:, q * wide : (q + 1) * wide]

    lane48 = lanes((48, 128))
    lane16 = lanes((16, 128))

    def pack_third(x, base):
        return jnp.where(
            lane48 < 32, turn(x[0:48], -base),
            jnp.where(lane48 < 64, turn(x[48:96], 32 - base), turn(x[96:144], 64 - base)),
        )

    def send_fine(slot):
        x = sent0[...]
        hs0[slot, 0] = pack_third(x, 32)
        hs0[slot, 1] = pack_third(x, 0)

    def send_middle(slot):
        x = sent1[:, 0:128]
        lower = x[0:80]
        upper = jnp.concatenate([x[80:144], jnp.zeros((16, 128), F32)], axis=0)
        left = lanes((80, 128)) < 64
        hs1[slot, 0] = jnp.where(left, turn(lower, 64), upper)
        hs1[slot, 1] = jnp.where(left, lower, turn(upper, 64))

    def send_group(send, recv, number, x, base):
        rows = slice(16 * number, 16 * number + 16)
        for j in range(N_SUB):
            acc = jnp.zeros((16, 128), F32)
            for q in range(9):
                piece = turn(x[16 * q : 16 * q + 16], 8 * q - base - 8 * j)
                acc = jnp.where((lane16 >= 8 * q) & (lane16 < 8 * q + 8), piece, acc)
            send[j, rows] = acc
        recv[sub, rows] = send[sub, rows]

    def take_group(recv, number, base):
        rows = slice(16 * number, 16 * number + 16)
        pieces = [recv[p, rows] for p in range(N_SUB)]
        found = []
        for q in range(9):
            acc = jnp.zeros((16, 128), F32)
            for p in range(N_SUB):
                at = base + 8 * p
                acc = jnp.where(
                    (lane16 >= at) & (lane16 < at + 8), turn(pieces[p], at - 8 * q), acc
                )
            found.append(acc)
        return jnp.concatenate(found, axis=0)

    def start(copies):
        for copy in copies:
            copy.start()

    def arrive(copies):
        for copy in copies:
            copy.wait_recv()

    def start_halo(copies):
        pl.when(jnp.logical_not(last))(copies[0].start)
        pl.when(jnp.logical_not(first))(copies[1].start)

    def arrive_halo(copies):
        pl.when(jnp.logical_not(first))(copies[0].wait_recv)
        pl.when(jnp.logical_not(last))(copies[1].wait_recv)

    def fine_ext(slot):
        below = hr0[slot, 0]
        above = hr0[slot, 1]
        found = []
        for r in range(3):
            found.append(
                jnp.where(
                    lane48 < 32, turn(below, -32 * r),
                    jnp.where(lane48 < 64, turn(above, 32 - 32 * r), base0[48 * r : 48 * r + 48]),
                )
            )
        store_ext(0, 0, jnp.concatenate(found, axis=0))

    def middle_ext(slot):
        below = hr1[slot, 0]
        above = hr1[slot, 1]
        left = lanes((80, 128)) < 64
        lower = jnp.where(left, below, turn(above, 64))
        upper = jnp.where(left, turn(below, 64), above)
        store_ext(1, 0, jnp.concatenate([lower, upper[0:64]], axis=0))

    fetched(0, 8, 9)
    load(0)
    send_table(0)
    traces(0)
    sum_a[...] = sent0[...]
    send_fine(0)
    pl.semaphore_wait(barrier, N_SUB - 1 + (me + total - 1) // total + 1 - (me + 1) // total)
    start_halo(halo_f[0])
    load(1)
    send_table(1)
    traces(1)
    send_middle(0)
    sum_b[...] = sent1[:, 128:256]
    send_group(gs0, gr0, 0, sent1[:, 128:256], 0)
    load(2)
    send_table(2)
    traces(2)
    send_group(gs0, gr0, 1, sent2[:, 256:384], 0)
    send_group(gs0, gr0, 2, sent2[:, 256:384], 32)
    hs2[0, 0] = sent2[:, 128:256]
    hs2[0, 1] = sent2[:, 0:128]
    start(group[0])
    start_halo(halo_m[0])
    start_halo(halo_c)
    fetched(1, 2, 3, 7, 6)
    coefficients(0)
    coefficients(1)
    coefficients(2)
    neighbour_table(0)
    volume(0)
    neighbour_table(1)
    volume(1)
    arrive(group[0])
    base0[...] = take_group(gr0, 0, 64) + take_group(gr0, 1, 96)
    start_mc = take_group(gr0, 2, 32)

    arrive_halo(halo_f[0])
    fine_ext(0)
    finish(0)
    traces(0)
    send_fine(1)
    start_halo(halo_f[1])
    sum_a[...] += sent0[...]
    send_group(gs1, gr1, 0, 0.5 * sum_a[...], 64)
    start(group[1])
    volume(0)
    neighbour_table(2)
    arrive_halo(halo_m[0])
    middle_ext(0)

    arrive_halo(halo_f[1])
    fine_ext(1)
    finish(0)
    traces(0)
    send_fine(2)
    start_halo(halo_f[2])
    sum_a[...] = 0.25 * sum_a[...] + 0.25 * sent0[...]
    base1 = sent0[...]
    volume(0)

    arrive(group[1])
    store_ext(1, 128, take_group(gr1, 0, 0) + start_mc)
    finish(1)
    traces(1)
    send_middle(1)
    start_halo(halo_m[1])
    send_group(gs2, gr2, 0, 0.5 * (sum_b[...] + sent1[:, 128:256]), 32)
    start(group[2])
    volume(1)

    arrive_halo(halo_f[2])
    fine_ext(2)
    finish(0)
    traces(0)
    send_fine(3)
    start_halo(halo_f[3])
    sum_a[...] += 0.25 * sent0[...]
    send_group(gs3, gr3, 0, 0.5 * (base1 + sent0[...]), 64)
    send_group(gs3, gr3, 1, sum_a[...], 96)
    start(group[3])
    volume(0)
    volume(2)
    arrive_halo(halo_c)
    store_ext(2, 0, hr2[0, 0])
    store_ext(2, 128, hr2[0, 1])
    arrive_halo(halo_m[1])
    middle_ext(1)

    arrive_halo(halo_f[3])
    fine_ext(3)
    finish(0)
    arrive(group[3])
    store_ext(1, 128, take_group(gr3, 0, 0) + start_mc)
    finish(1)
    arrive(group[2])
    store_ext(2, 256, take_group(gr3, 1, 0) + take_group(gr2, 0, 32))
    finish(2)
    for q in range(9):
        out[q, :, 0:64] = u0[q, 0:35, 0:64]
        out[q, :, 64:192] = u1[q, 0:35, :]
        out[q, :, 192:448] = u2[q, 0:35, :]
    for copies in halo_f + halo_m + [halo_c]:
        pl.when(jnp.logical_not(last))(copies[0].wait_send)
        pl.when(jnp.logical_not(first))(copies[1].wait_send)
    for copies in group:
        for copy in copies:
            copy.wait_send()


def scratch(held):
    shapes = [pltpu.VMEM(x.shape, x.dtype) for x in held]
    shapes += [pltpu.SemaphoreType.DMA((len(held),))]
    shapes += [pltpu.VMEM((9, 40, w), F32) for w in WIDE] * 2
    shapes += [pltpu.VMEM((288, o + e), BF16) for o, e in zip(OWN, EXT)]
    shapes += [pltpu.VMEM((144, o), F32) for o in OWN]
    shapes += [pltpu.VMEM((144, 9 * 256), BF16)] + [pltpu.VMEM((248, 9 * w), F32) for w in WIDE]
    shapes += [pltpu.VMEM((2, 256, 9 * 256), BF16)]
    shapes += [pltpu.VMEM((o + e, o), BF16) for o, e in zip(OWN, EXT)]
    shapes += [pltpu.VMEM((o, s), BF16) for o, s in zip(OWN, SENT)]
    shapes += [pltpu.VMEM((32, w), F32) for w in WIDE]
    shapes += [pltpu.VMEM((1, o), F32) for o in OWN]
    shapes += [pltpu.VMEM((3, 16, o), BF16) for o in OWN]
    shapes += [pltpu.VMEM((3, 40, 128), F32), pltpu.VMEM((48, 128), F32)]
    shapes += [pltpu.VMEM((248, 144), BF16), pltpu.VMEM((96, 256), BF16)]
    shapes += [pltpu.VMEM((144, s), F32) for s in SENT]
    shapes += [pltpu.VMEM((144, 128), F32)] * 3
    shapes += [pltpu.VMEM((4, 2, 48, 128), F32)] * 2
    shapes += [pltpu.VMEM((2, 2, 80, 128), F32)] * 2
    shapes += [pltpu.VMEM((1, 2, 144, 128), F32)] * 2
    for buffers in (3, 1, 1, 2):
        shapes += [pltpu.VMEM((N_SUB, 16 * buffers, 128), F32)] * 2
    for slots in (4, 2, 1):
        shapes += [pltpu.SemaphoreType.DMA((slots, 2))] * 2
    shapes += [pltpu.SemaphoreType.DMA((4, 4))] * 2
    return shapes


def solution(mesh):
    n_dom = mesh.shape["dom"]
    place, select, spread = constants()

    def on_device(*arrays):
        held = arrays[:-1] + (
            arrays[-1].transpose(1, 0, 2),
            jnp.asarray(place, BF16), jnp.asarray(select, F32), jnp.asarray(spread, BF16),
        )
        return pl.pallas_call(
            functools.partial(kernel, n_dom),
            out_shape=pltpu.VMEM(arrays[0].shape, F32),
            in_specs=[pl.BlockSpec(memory_space=pltpu.HBM)] * 13,
            out_specs=pl.BlockSpec(memory_space=pltpu.VMEM),
            scratch_shapes=scratch(held),
            compiler_params=pltpu.CompilerParams(
                collective_id=0, has_side_effects=True, vmem_limit_bytes=60 * 1024 * 1024
            ),
            name="step",
        )(*held)

    split_all = ("dom", "sub")
    placed = (
        P(None, None, split_all), P(None, split_all), P(None, None, split_all),
        P(None, split_all), P(), P(), P(None, split_all), P(None, split_all),
        P(None, split_all), P(None, None, split_all),
    )
    return jax.shard_map(
        on_device, mesh=mesh, in_specs=placed, out_specs=P(None, None, split_all), check_vma=False,
    )
```

```python
import functools

import jax
import jax.numpy as jnp
import numpy as np
from jax import lax
from jax.experimental import pallas as pl
from jax.experimental.pallas import tpu as pltpu
from jax.sharding import PartitionSpec as P

F32 = jnp.float32
BF16 = jnp.bfloat16
MESH = pl.DeviceIdType.MESH
N_SUB = 4
COARSE_STEP = 0.1

LANE = (0, 64, 192)
WIDE = (128, 128, 256)
OWN = (512, 512, 1024)
EXT = (128, 256, 384)
SENT = (128, 256, 256)
STEP = (COARSE_STEP / 4, COARSE_STEP / 2, COARSE_STEP)

VOIGT = ((3, 8, 7), (8, 4, 6), (7, 6, 5))


def face_tables():
    lattice = [
        (a, b, c, 4 - a - b - c) for a in range(5) for b in range(5 - a) for c in range(5 - a - b)
    ]
    face_rows = np.array(
        [[i for i, p in enumerate(lattice) if p[f] == 0] for f in range(4)], np.int32
    )
    triangle = [p[1:] for p in lattice if p[0] == 0]
    position = {p: i for i, p in enumerate(triangle)}

    def turned(p, times):
        p = (p[1], p[0], p[2])
        for _ in range(times):
            p = (p[1], p[2], p[0])
        return p

    orders = np.array(
        [[position[turned(p, o)] for p in triangle] for o in range(3)], np.int32
    )
    return face_rows, orders


def constants():
    face_rows, orders = face_tables()
    place = np.zeros((2, 128, 144), np.float32)
    for n in range(35):
        place[0, n, n] = 1
        place[0, n, 48 + n] = 1
        place[1, n, 96 + n] = 1
    select = np.zeros((128, 144), np.float32)
    for f in range(4):
        for n in range(15):
            select[f * 16 + n, face_rows[f, n]] = 1
            select[64 + f * 16 + n, 48 + face_rows[f, n]] = 1
    spread = np.zeros((128, 256), np.float32)
    for f in range(4):
        for n in range(15):
            for o in range(3):
                spread[f * 15 + n, (o * 4 + f) * 16 + orders[o, n]] = 1
            spread[f * 15 + n, 192 + f * 16 + n] = -1
    return place, select, spread


def split(x):
    high = x.astype(BF16)
    return high, (x - high.astype(F32)).astype(BF16)


def dot(a, b):
    return jnp.dot(a, b, preferred_element_type=F32)


def lanes(shape):
    return lax.broadcasted_iota(jnp.int32, shape, 1)


def turn(x, shift):
    shift %= 128
    return pltpu.roll(x, shift, 1) if shift else x


def fill_one_hot(ref, columns, indices, base=0):
    chunk = 32
    for start in range(0, ref.shape[0], chunk):
        iota = lax.broadcasted_iota(jnp.int32, (chunk, indices[0].shape[1]), 0)
        hit = None
        for index in indices:
            here = iota == jnp.broadcast_to(index - (base + start), iota.shape)
            hit = here if hit is None else hit | here
        ref[start : start + chunk, columns] = jnp.where(hit, 1.0, 0.0).astype(BF16)


def kernel(
    n_dom,
    *refs,
):
    ins, out, held, in_sems, rest = refs[:13], refs[13], refs[14:27], refs[27], refs[28:]
    body(n_dom, ins, in_sems, out, *held, *rest)


def body(
    n_dom, ins, in_sems, out,
    wave, mat, geo, fs, der, lift, nbr, ori, halo, iface, place, select, spread,
    u0, u1, u2, v0, v1, v2, t0, t1, t2, g0, g1, g2,
    stack0, stack1, stack2, stack3, prod0, prod1, prod2, jump, xj0, xj1, xj2,
    oh0, oh1, oh2, xx0, xx1, xx2, xm0, xm1, xm2, xs0, xs1, xs2,
    os0, os1, os2, cf0, cf1, cf2, sc0, sc1, sc2, om0, om1, om2,
    ix0, ix1, ix2, row_of, xtab, dpad, lpad, amat, smat, emat, lmat, sent0, sent1, sent2, sum_a, sum_b, base0,
    hs0, hr0, hs1, hr1, hs2, hr2, gs0, gr0, gs1, gr1, gs2, gr2, gs3, gr3, gs4, gr4,
    ss0, rs0, ss1, rs1, ss2, rs2, gss, grs,
):
    us, vs, ts, gs_, ohs, oss = (u0, u1, u2), (v0, v1, v2), (t0, t1, t2), (g0, g1, g2), (oh0, oh1, oh2), (os0, os1, os2)
    cfs, scs, oms, sents = (cf0, cf1, cf2), (sc0, sc1, sc2), (om0, om1, om2), (sent0, sent1, sent2)
    prods, stacks, xjs = (prod0, prod1, prod2), (stack0, stack1, stack2), (xj0, xj1, xj2)
    xxs, xms, xss = (xx0, xx1, xx2), (xm0, xm1, xm2), (xs0, xs1, xs2)
    total = n_dom * N_SUB
    dom = lax.axis_index("dom")
    sub = lax.axis_index("sub")
    me = dom * N_SUB + sub
    up = (me + 1) % total
    down = (me + total - 1) % total
    up_id = (up // N_SUB, up % N_SUB)
    down_id = (down // N_SUB, down % N_SUB)
    first, last = me == 0, me == total - 1

    barrier = pltpu.get_barrier_semaphore()

    @pl.when(jnp.logical_not(last))
    def _():
        pl.semaphore_signal(barrier, inc=1, device_id=up_id, device_id_type=MESH)

    @pl.when(jnp.logical_not(first))
    def _():
        pl.semaphore_signal(barrier, inc=1, device_id=down_id, device_id_type=MESH)

    for k in range(1, N_SUB):
        pl.semaphore_signal(
            barrier, inc=1, device_id=(dom, (sub + k) % N_SUB), device_id_type=MESH
        )

    def halo_copies(send, recv, ssem, rsem, slot):
        return [
            pltpu.make_async_remote_copy(
                src_ref=send.at[slot, way], dst_ref=recv.at[slot, way],
                send_sem=ssem.at[slot, way], recv_sem=rsem.at[slot, way],
                device_id=(up_id, down_id)[way], device_id_type=MESH,
            )
            for way in range(2)
        ]

    def group_copies(send, recv, number):
        found = []
        for k in range(1, N_SUB):
            dest = (sub + k) % N_SUB
            found.append(
                pltpu.make_async_remote_copy(
                    src_ref=send.at[dest], dst_ref=recv.at[sub],
                    send_sem=gss.at[number, k], recv_sem=grs.at[number, k],
                    device_id=(dom, dest), device_id_type=MESH,
                )
            )
        return found

    held = (wave, mat, geo, fs, der, lift, nbr, ori, halo, iface, place, select, spread)
    fetch = {
        i: pltpu.make_async_copy(ins[i], held[i], in_sems.at[i])
        for i in (4, 5, 10, 11, 12, 0, 8, 9, 1, 2, 3, 7, 6)
    }
    for copy in fetch.values():
        copy.start()

    def fetched(*numbers):
        for i in numbers:
            fetch[i].wait()

    for end, way in ((first, 0), (last, 1)):

        @pl.when(end)
        def _():
            for ref in (hr0, hr1, hr2):
                ref[:, way] = jnp.zeros((ref.shape[0],) + ref.shape[2:], F32)

    halo_f = [halo_copies(hs0, hr0, ss0, rs0, s) for s in range(4)]
    halo_m = [halo_copies(hs1, hr1, ss1, rs1, s) for s in range(2)]
    halo_c = halo_copies(hs2, hr2, ss2, rs2, 0)
    group = [
        group_copies(s, r, i)
        for i, (s, r) in enumerate(((gs0, gr0), (gs1, gr1), (gs2, gr2), (gs3, gr3), (gs4, gr4)))
    ]

    dpad[...] = jnp.zeros_like(dpad)
    lpad[...] = jnp.zeros_like(lpad)
    fetched(4, 5, 10, 11, 12)
    for k in range(3):
        dpad[k, 0:35, 0:35] = der[k]
    lpad[0:35, 0:60] = lift[...]
    parts = []
    for k in range(3):
        high, low = split(dpad[k])
        parts.append(dot(high, place[0]) + dot(low, place[1]))
    amat[...] = jnp.concatenate(parts, axis=0).astype(BF16)
    smat[...] = select[:, 0:96].astype(BF16)
    emat[...] = (select[0:64, 0:96] + select[64:128, 0:96]).astype(BF16)
    high, low = split(lpad[...])
    lmat[0:48] = dot(high, spread[...]).astype(BF16)
    lmat[48:96] = dot(low, spread[...]).astype(BF16)

    def remap(index, c):
        if c:
            return index
        return jnp.where(
            index < 256, (index & 63) + ((index >> 6) << 7), index + 256
        )

    def load(c):
        first, wide = LANE[c], WIDE[c]
        span = slice(first, first + wide)
        u = us[c]
        for q in range(9):
            u[q, 32:40, :] = jnp.zeros((8, wide), F32)
            u[q, 0:35, :] = wave[q, :, span]

    def coefficients(c):
        first, wide = LANE[c], WIDE[c]
        span = slice(first, first + wide)
        rho = STEP[c] / mat[0:1, span]
        lam = STEP[c] * mat[1:2, span]
        mu = STEP[c] * mat[2:3, span]
        cf = cfs[c]
        for i in range(3):
            axes = geo[i, :, span]
            cf[3 * i : 3 * i + 3] = axes * mu
            cf[9 + 3 * i : 12 + 3 * i] = axes * rho
            cf[18 + 3 * i : 21 + 3 * i] = axes
        cf[27:28] = lam
        cf[28:29] = 2.0 * mu
        for f in range(4):
            where = slice(f * wide, (f + 1) * wide)
            scs[c][:, where] = (0.5 * STEP[c]) * fs[f : f + 1, span]
            row = jnp.broadcast_to(ori[f : f + 1, span], (16, wide))
            for o in range(3):
                oms[c][o, :, where] = jnp.where(row == o, 1.0, 0.0).astype(BF16)

    def send_table(c):
        blank = jnp.full((1, 64), -1, jnp.int32)
        if c == 0:
            rows = [(halo[0:1, 0:32], halo[1:2, 0:32], iface[0, 0:1], iface[1, 0:1])]
        elif c == 1:
            rows = [(halo[0:1, 32:96], halo[1:2, 32:96]), (iface[0, 1:2], iface[2, 0:1], blank)]
        else:
            rows = [(halo[0:1, 96:224],), (halo[1:2, 96:224],)]
        for i, row in enumerate(rows):
            at = slice(3 * c + i, 3 * c + i + 1)
            row_of[at] = remap(jnp.concatenate(row, axis=1), c)
            fill_one_hot(oss[c], slice(128 * i, 128 * i + 128), [row_of[at]])

    def neighbour_table(c):
        wide, own, ext = WIDE[c], OWN[c], EXT[c]
        span = slice(LANE[c], LANE[c] + wide)
        index = remap(nbr[:, span], c)
        if c == 0:
            index = jnp.where(lanes(index.shape) < 64, index, -1)
        ixs = (ix0, ix1, ix2)[c]
        ixs[...] = jnp.full((8, wide), -1, jnp.int32)
        ixs[0:4] = index
        upright = (ixs[...] - own).astype(F32).T
        across = lanes((32, ext)).astype(F32)
        scale_at = None
        for f in range(4):
            face = slice(f * wide, (f + 1) * wide)
            fill_one_hot(ohs[c], face, [ixs[f : f + 1]])
            high, low = split(jnp.broadcast_to(scs[c][:, face], (16, wide)))
            tall = jnp.concatenate([oms[c][o, :, face] for o in range(3)] + [high, low], axis=0)
            for start in range(0, wide, 32):
                column = jnp.broadcast_to(upright[start : start + 32, f : f + 1], (32, ext))
                xtab[start : start + 32, 0:ext] = jnp.where(column == across, 1.0, 0.0).astype(BF16)
            found = dot(tall, xtab[0:wide, 0:ext])
            for o in range(3):
                xms[c][4 * o + f] = found[16 * o : 16 * o + 16].astype(BF16)
            both = found[48:64] + found[64:80]
            scale_at = both if scale_at is None else scale_at + both
        fill_one_hot(xxs[c], slice(0, wide), [ixs[f : f + 1] for f in range(4)], own)
        xss[c][...] = scale_at

    def early(c, row):
        wide = WIDE[c]
        at = slice(2 * c - 1, 2 * c)
        row_of[at] = row
        row = row_of[at]
        element, face = row & (wide - 1), row >> (7 if c == 1 else 8)
        tall = jnp.concatenate([us[c][q] for q in range(9)], axis=0)
        high = tall.astype(BF16).astype(F32)
        both = jnp.concatenate([high, tall - high], axis=0).astype(BF16)
        fill_one_hot(xtab.at[0:wide], slice(0, 128), [element])
        picked = dot(both, xtab[0:wide, 0:128])
        gap = jnp.zeros((8, 128), F32)
        for q in range(9):
            pair = [picked[40 * q : 40 * q + 40], gap, picked[360 + 40 * q : 400 + 40 * q], gap]
            stack3[:, 128 * q : 128 * q + 128] = jnp.concatenate(pair, axis=0).astype(BF16)
        nodes = dot(emat[...], stack3[...])
        face = jnp.broadcast_to(face, (16, 128))
        found = []
        for q in range(9):
            span = slice(128 * q, 128 * q + 128)
            acc = jnp.zeros((16, 128), F32)
            for f in range(4):
                acc = jnp.where(face == f, nodes[16 * f : 16 * f + 16, span], acc)
            found.append(acc)
        return jnp.concatenate(found, axis=0)

    def traces(c):
        wide = WIDE[c]
        u, t, stack = us[c], ts[c], stacks[c]
        gap = jnp.zeros((8, wide), F32)
        for q in range(9):
            x = u[q]
            high = x.astype(BF16).astype(F32)
            tall = jnp.concatenate([high, gap, x - high, gap, high, gap], axis=0)
            stack[:, q * wide : (q + 1) * wide] = tall.astype(BF16)
        picked = dot(smat[...], stack[0:96])
        for q in range(9):
            where = slice(q * wide, (q + 1) * wide)
            for part in range(2):
                for f in range(4):
                    row = 64 * part + 16 * f
                    t[144 * part + 16 * q : 144 * part + 16 * q + 16, f * wide : (f + 1) * wide] = (
                        picked[row : row + 16, where].astype(BF16)
                    )
        both = dot(t[...], oss[c][...])
        sents[c][...] = both[0:144] + both[144:288]

    def volume(c):
        wide = WIDE[c]
        cf, prod, t = cfs[c], prods[c], ts[c]
        prod[...] = dot(amat[...], stacks[c][...])
        both = dot(t[...], ohs[c][...])
        gs_[c][...] = both[0:144] + both[144:288]
        scale = scs[c][...]
        for q in range(9):
            rows = slice(16 * q, 16 * q + 16)
            low_rows = slice(144 + 16 * q, 160 + 16 * q)
            high, low = split(gs_[c][rows] * scale)
            mine = t[rows].astype(F32) + t[low_rows].astype(F32)
            own_high, own_low = split(mine * scale)
            where = slice(q * wide, (q + 1) * wide)
            for f in range(4):
                face = slice(f * wide, (f + 1) * wide)
                for o in range(3):
                    mask = oms[c][o, :, face]
                    at = (4 * o + f) * 16
                    jump[0, at : at + 16, where] = high[:, face] * mask
                    jump[1, at : at + 16, where] = low[:, face] * mask
                at = 192 + 16 * f
                jump[0, at : at + 16, where] = own_high[:, face]
                jump[1, at : at + 16, where] = own_low[:, face]
        first = dot(lmat[...], jump[0, :, 0 : 9 * wide])
        second = dot(lmat[0:48], jump[1, :, 0 : 9 * wide])
        whole = first[0:40] + first[48:88] + second[0:40]
        for start in range(0, wide, 128):
            span = slice(start, start + 128)

            def old(q):
                at = q * wide + start
                return us[c][q, :, span] + whole[:, at : at + 128]

            def grad(q, i, kind):
                at = q * wide + start
                base = 9 * kind + 3 * i
                return sum(
                    jnp.broadcast_to(cf[base + k : base + k + 1, span], (40, 128))
                    * prod[40 * k : 40 * k + 40, at : at + 128]
                    for k in range(3)
                )

            for i in range(3):
                rate = grad(VOIGT[i][0], 0, 1) + grad(VOIGT[i][1], 1, 1) + grad(VOIGT[i][2], 2, 1)
                vs[c][i, :, span] = old(i) + rate
            diag = [grad(i, i, 2) for i in range(3)]
            shared = cf[27:28, span] * (diag[0] + diag[1] + diag[2])
            for i in range(3):
                vs[c][3 + i, :, span] = old(3 + i) + (shared + cf[28:29, span] * diag[i])
            for q, i, j in ((6, 1, 2), (7, 0, 2), (8, 0, 1)):
                rate = grad(j, i, 0) + grad(i, j, 0)
                vs[c][q, :, span] = old(q) + rate

    def receive(c, tile, value, new=False):
        span = slice(128 * tile, 128 * tile + 128)
        xj = xjs[c]
        scale = xss[c][:, span]
        for q in range(9):
            high, low = split(value[16 * q : 16 * q + 16] * scale)
            where = slice(128 * q, 128 * q + 128)
            for i in range(12):
                mask = xms[c][i, :, span]
                xj[0, 16 * i : 16 * i + 16, where] = high * mask
                xj[1, 16 * i : 16 * i + 16, where] = low * mask
        first = dot(lmat[:, 0:192], xj[0])
        second = dot(lmat[0:48, 0:192], xj[1])
        whole = first[0:40] + first[48:88] + second[0:40]
        tall = jnp.concatenate([whole[:, 128 * q : 128 * q + 128] for q in range(9)], axis=0)
        high = tall.astype(BF16).astype(F32)
        both = jnp.concatenate([high, tall - high], axis=0).astype(BF16)
        added = dot(both, xxs[c][span])
        target = us[c] if new else vs[c]
        for q in range(9):
            at = 40 * q
            target[q] = vs[c][q] + (added[at : at + 40] + added[360 + at : 400 + at])

    lane48 = lanes((48, 128))
    lane16 = lanes((16, 128))

    def pack_third(x, base):
        return jnp.where(
            lane48 < 32, turn(x[0:48], -base),
            jnp.where(lane48 < 64, turn(x[48:96], 32 - base), turn(x[96:144], 64 - base)),
        )

    def send_fine(slot):
        x = sent0[...]
        hs0[slot, 0] = pack_third(x, 32)
        hs0[slot, 1] = pack_third(x, 0)

    def send_middle(slot):
        x = sent1[:, 0:128]
        lower = x[0:80]
        upper = jnp.concatenate([x[80:144], jnp.zeros((16, 128), F32)], axis=0)
        left = lanes((80, 128)) < 64
        hs1[slot, 0] = jnp.where(left, turn(lower, 64), upper)
        hs1[slot, 1] = jnp.where(left, lower, turn(upper, 64))

    def send_group(send, recv, number, x, base):
        rows = slice(16 * number, 16 * number + 16)
        for j in range(N_SUB):
            acc = jnp.zeros((16, 128), F32)
            for q in range(9):
                piece = turn(x[16 * q : 16 * q + 16], 8 * q - base - 8 * j)
                acc = jnp.where((lane16 >= 8 * q) & (lane16 < 8 * q + 8), piece, acc)
            send[j, rows] = acc
        recv[sub, rows] = send[sub, rows]

    def take_group(recv, number, base):
        rows = slice(16 * number, 16 * number + 16)
        pieces = [recv[p, rows] for p in range(N_SUB)]
        found = []
        for q in range(9):
            acc = jnp.zeros((16, 128), F32)
            for p in range(N_SUB):
                at = base + 8 * p
                acc = jnp.where(
                    (lane16 >= at) & (lane16 < at + 8), turn(pieces[p], at - 8 * q), acc
                )
            found.append(acc)
        return jnp.concatenate(found, axis=0)

    def start(copies):
        for copy in copies:
            copy.start()

    def arrive(copies):
        for copy in copies:
            copy.wait_recv()

    def start_halo(copies):
        pl.when(jnp.logical_not(last))(copies[0].start)
        pl.when(jnp.logical_not(first))(copies[1].start)

    def arrive_halo(copies):
        pl.when(jnp.logical_not(first))(copies[0].wait_recv)
        pl.when(jnp.logical_not(last))(copies[1].wait_recv)

    def fine_halo(slot):
        below = hr0[slot, 0]
        above = hr0[slot, 1]
        found = []
        for r in range(3):
            found.append(
                jnp.where(
                    lane48 < 32, turn(below, -32 * r),
                    jnp.where(lane48 < 64, turn(above, 32 - 32 * r), base0[48 * r : 48 * r + 48]),
                )
            )
        receive(0, 0, jnp.concatenate(found, axis=0), new=True)

    def middle_halo(slot):
        below = hr1[slot, 0]
        above = hr1[slot, 1]
        left = lanes((80, 128)) < 64
        lower = jnp.where(left, below, turn(above, 64))
        upper = jnp.where(left, turn(below, 64), above)
        receive(1, 0, jnp.concatenate([lower, upper[0:64]], axis=0))

    fetched(0, 8, 9)
    load(0)
    send_table(0)
    traces(0)
    sum_a[...] = sent0[...]
    send_fine(0)
    pl.semaphore_wait(barrier, N_SUB - 1 + (me + total - 1) // total + 1 - (me + 1) // total)
    start_halo(halo_f[0])
    load(1)
    load(2)
    blank = jnp.full((1, 64), -1, jnp.int32)
    start_m = early(1, jnp.concatenate([iface[0, 1:2], iface[2, 0:1], blank], axis=1))
    start_c = early(2, jnp.concatenate([iface[1, 1:2], iface[2, 1:2], blank], axis=1))
    sum_b[...] = start_m
    send_group(gs0, gr0, 0, start_m, 0)
    send_group(gs0, gr0, 1, start_c, 0)
    start(group[0])
    send_group(gs4, gr4, 0, start_c, 32)
    start(group[4])
    send_table(1)
    traces(1)
    send_middle(0)
    start_halo(halo_m[0])
    send_table(2)
    traces(2)
    hs2[0, 0] = sent2[:, 128:256]
    hs2[0, 1] = sent2[:, 0:128]
    start_halo(halo_c)
    fetched(1, 2, 3, 7, 6)
    coefficients(0)
    neighbour_table(0)
    volume(0)
    coefficients(1)
    coefficients(2)
    neighbour_table(1)
    arrive(group[0])
    base0[...] = take_group(gr0, 0, 64) + take_group(gr0, 1, 96)

    arrive_halo(halo_f[0])
    fine_halo(0)
    traces(0)
    send_fine(1)
    start_halo(halo_f[1])
    sum_a[...] += sent0[...]
    send_group(gs1, gr1, 0, 0.5 * sum_a[...], 64)
    start(group[1])
    volume(0)
    volume(1)
    arrive_halo(halo_m[0])
    middle_halo(0)
    arrive(group[4])
    start_mc = take_group(gr4, 0, 32)
    neighbour_table(2)

    arrive_halo(halo_f[1])
    fine_halo(1)
    traces(0)
    send_fine(2)
    start_halo(halo_f[2])
    sum_a[...] = 0.25 * sum_a[...] + 0.25 * sent0[...]
    base1 = sent0[...]
    volume(0)

    arrive(group[1])
    receive(1, 1, take_group(gr1, 0, 0) + start_mc, new=True)
    traces(1)
    send_middle(1)
    start_halo(halo_m[1])
    send_group(gs2, gr2, 0, 0.5 * (sum_b[...] + sent1[:, 128:256]), 32)
    start(group[2])
    volume(2)

    arrive_halo(halo_f[2])
    fine_halo(2)
    traces(0)
    send_fine(3)
    start_halo(halo_f[3])
    sum_a[...] += 0.25 * sent0[...]
    send_group(gs3, gr3, 0, 0.5 * (base1 + sent0[...]), 64)
    send_group(gs3, gr3, 1, sum_a[...], 96)
    start(group[3])
    volume(0)
    volume(1)
    arrive_halo(halo_m[1])
    middle_halo(1)
    arrive_halo(halo_c)
    receive(2, 0, hr2[0, 0])
    receive(2, 1, hr2[0, 1])
    arrive(group[2])
    mean = take_group(gr2, 0, 32)

    arrive_halo(halo_f[3])
    arrive(group[3])
    fine_halo(3)
    receive(1, 1, take_group(gr3, 0, 0) + start_mc, new=True)
    receive(2, 2, take_group(gr3, 1, 0) + mean, new=True)
    for q in range(9):
        out[q, :, 0:64] = u0[q, 0:35, 0:64]
        out[q, :, 64:192] = u1[q, 0:35, :]
        out[q, :, 192:448] = u2[q, 0:35, :]
    for copies in halo_f + halo_m + [halo_c]:
        pl.when(jnp.logical_not(last))(copies[0].wait_send)
        pl.when(jnp.logical_not(first))(copies[1].wait_send)
    for copies in group:
        for copy in copies:
            copy.wait_send()


def scratch(held):
    shapes = [pltpu.VMEM(x.shape, x.dtype) for x in held]
    shapes += [pltpu.SemaphoreType.DMA((len(held),))]
    shapes += [pltpu.VMEM((9, 40, w), F32) for w in WIDE] * 2
    shapes += [pltpu.VMEM((288, o), BF16) for o in OWN]
    shapes += [pltpu.VMEM((144, o), F32) for o in OWN]
    shapes += [pltpu.VMEM((144, 9 * w), BF16) for w in WIDE] + [pltpu.VMEM((96, 9 * 128), BF16)]
    shapes += [pltpu.VMEM((120, 9 * w), F32) for w in WIDE]
    shapes += [pltpu.VMEM((2, 256, 9 * 256), BF16)]
    shapes += [pltpu.VMEM((2, 192, 9 * 128), BF16)] * 3
    shapes += [pltpu.VMEM((o, o), BF16) for o in OWN]
    shapes += [pltpu.VMEM((e, w), BF16) for e, w in zip(EXT, WIDE)]
    shapes += [pltpu.VMEM((12, 16, e), BF16) for e in EXT]
    shapes += [pltpu.VMEM((16, e), F32) for e in EXT]
    shapes += [pltpu.VMEM((o, s), BF16) for o, s in zip(OWN, SENT)]
    shapes += [pltpu.VMEM((32, w), F32) for w in WIDE]
    shapes += [pltpu.VMEM((1, o), F32) for o in OWN]
    shapes += [pltpu.VMEM((3, 16, o), BF16) for o in OWN]
    shapes += [pltpu.VMEM((8, w), jnp.int32) for w in WIDE] + [pltpu.VMEM((8, 128), jnp.int32)]
    shapes += [pltpu.VMEM((256, 384), BF16)]
    shapes += [pltpu.VMEM((3, 40, 128), F32), pltpu.VMEM((48, 128), F32)]
    shapes += [pltpu.VMEM((120, 144), BF16), pltpu.VMEM((128, 96), BF16)]
    shapes += [pltpu.VMEM((64, 96), BF16), pltpu.VMEM((96, 256), BF16)]
    shapes += [pltpu.VMEM((144, s), F32) for s in SENT]
    shapes += [pltpu.VMEM((144, 128), F32)] * 3
    shapes += [pltpu.VMEM((4, 2, 48, 128), F32)] * 2
    shapes += [pltpu.VMEM((2, 2, 80, 128), F32)] * 2
    shapes += [pltpu.VMEM((1, 2, 144, 128), F32)] * 2
    for buffers in (2, 1, 1, 2, 1):
        shapes += [pltpu.VMEM((N_SUB, 16 * buffers, 128), F32)] * 2
    for slots in (4, 2, 1):
        shapes += [pltpu.SemaphoreType.DMA((slots, 2))] * 2
    shapes += [pltpu.SemaphoreType.DMA((5, 4))] * 2
    return shapes


def solution(mesh):
    n_dom = mesh.shape["dom"]
    place, select, spread = constants()

    def on_device(*arrays):
        held = arrays[:-1] + (
            arrays[-1].transpose(1, 0, 2),
            jnp.asarray(place, BF16), jnp.asarray(select, F32), jnp.asarray(spread, BF16),
        )
        return pl.pallas_call(
            functools.partial(kernel, n_dom),
            out_shape=pltpu.VMEM(arrays[0].shape, F32),
            in_specs=[pl.BlockSpec(memory_space=pltpu.HBM)] * 13,
            out_specs=pl.BlockSpec(memory_space=pltpu.VMEM),
            scratch_shapes=scratch(held),
            compiler_params=pltpu.CompilerParams(
                collective_id=0, has_side_effects=True, vmem_limit_bytes=60 * 1024 * 1024
            ),
            name="step",
        )(*held)

    split_all = ("dom", "sub")
    placed = (
        P(None, None, split_all), P(None, split_all), P(None, None, split_all),
        P(None, split_all), P(), P(), P(None, split_all), P(None, split_all),
        P(None, split_all), P(None, None, split_all),
    )
    return jax.shard_map(
        on_device, mesh=mesh, in_specs=placed, out_specs=P(None, None, split_all), check_vma=False,
    )
```

```python
import functools

import jax
import jax.numpy as jnp
import numpy as np
from jax import lax
from jax.experimental import pallas as pl
from jax.experimental.pallas import tpu as pltpu
from jax.sharding import PartitionSpec as P

F32 = jnp.float32
BF16 = jnp.bfloat16
MESH = pl.DeviceIdType.MESH
N_SUB = 4
COARSE_STEP = 0.1

LANE = (0, 64, 192)
WIDE = (128, 128, 256)
OWN = (512, 512, 1024)
EXT = (128, 256, 384)
SENT = (128, 256, 256)
STEP = (COARSE_STEP / 4, COARSE_STEP / 2, COARSE_STEP)

VOIGT = ((3, 8, 7), (8, 4, 6), (7, 6, 5))


def face_tables():
    lattice = [
        (a, b, c, 4 - a - b - c) for a in range(5) for b in range(5 - a) for c in range(5 - a - b)
    ]
    face_rows = np.array(
        [[i for i, p in enumerate(lattice) if p[f] == 0] for f in range(4)], np.int32
    )
    triangle = [p[1:] for p in lattice if p[0] == 0]
    position = {p: i for i, p in enumerate(triangle)}

    def turned(p, times):
        p = (p[1], p[0], p[2])
        for _ in range(times):
            p = (p[1], p[2], p[0])
        return p

    orders = np.array(
        [[position[turned(p, o)] for p in triangle] for o in range(3)], np.int32
    )
    return face_rows, orders


def constants():
    face_rows, orders = face_tables()
    place = np.zeros((2, 128, 144), np.float32)
    for n in range(35):
        place[0, n, n] = 1
        place[0, n, 48 + n] = 1
        place[1, n, 96 + n] = 1
    select = np.zeros((128, 144), np.float32)
    for f in range(4):
        for n in range(15):
            select[f * 16 + n, face_rows[f, n]] = 1
            select[64 + f * 16 + n, 48 + face_rows[f, n]] = 1
    spread = np.zeros((2, 128, 128), np.float32)
    for f in range(4):
        for n in range(15):
            spread[0, f * 15 + n, f * 16 + n] = 1
            spread[0, f * 15 + n, 64 + f * 16 + n] = 1
            spread[1, f * 15 + n, f * 16 + n] = 1
    turns = np.full((3, 16, 128), 15, np.int32)
    turns[:, :15] = orders[:, :, None]
    return place, select, spread, turns


def split(x):
    high = x.astype(BF16)
    return high, (x - high.astype(F32)).astype(BF16)


def dot(a, b):
    return jnp.dot(a, b, preferred_element_type=F32)


def lanes(shape):
    return lax.broadcasted_iota(jnp.int32, shape, 1)


def turn(x, shift):
    shift %= 128
    return pltpu.roll(x, shift, 1) if shift else x


def put(ref, rows, tile, value):
    for i in range(value.shape[1] // 128):
        ref[tile + i, rows, :] = value[:, 128 * i : 128 * i + 128]


def get(ref, rows=slice(None), start=0, stop=None):
    stop = ref.shape[0] if stop is None else stop
    return jnp.concatenate([ref[i, rows, :] for i in range(start, stop)], axis=1)


def fill_one_hot(ref, tile, indices, base=0, rows=None):
    chunk = 32
    for start in range(0, rows or ref.shape[1], chunk):
        iota = lax.broadcasted_iota(jnp.int32, (chunk, indices[0].shape[1]), 0)
        hit = None
        for index in indices:
            here = iota == jnp.broadcast_to(index - (base + start), iota.shape)
            hit = here if hit is None else hit | here
        put(ref, slice(start, start + chunk), tile, jnp.where(hit, 1.0, 0.0).astype(BF16))


def kernel(
    n_dom,
    *refs,
):
    ins, out, held, in_sems, rest = refs[:14], refs[14], refs[15:29], refs[29], refs[30:]
    body(n_dom, ins, in_sems, out, *held, *rest)


def body(
    n_dom, ins, in_sems, out,
    wave, mat, geo, fs, der, lift, nbr, ori, halo, iface, place, select, spread, turns,
    u0, u1, u2, v0, v1, v2, t0, t1, t2, g0, g1, g2,
    stack0, stack1, stack2, stack3, prod0, prod1, prod2, jump, xj0, xj1, xj2,
    oh0, oh1, oh2, xx0, xx1, xx2, xm0, xm1, xm2, xs0, xs1, xs2,
    xi0, xi1, xi2, tn0, tn1, tn2,
    os0, os1, os2, cf0, cf1, cf2, sc0, sc1, sc2, om0, om1, om2,
    ix0, ix1, ix2, row_of, xtab, dpad, lpad, amat, smat, emat, lmat, sent0, sent1, sent2, sum_a, sum_b, base0,
    hs0, hr0, hs1, hr1, hs2, hr2, gs0, gr0, gs1, gr1, gs2, gr2, gs3, gr3, gs4, gr4,
    ss0, rs0, ss1, rs1, ss2, rs2, gss, grs,
):
    us, vs, ts, gs_, ohs, oss = (u0, u1, u2), (v0, v1, v2), (t0, t1, t2), (g0, g1, g2), (oh0, oh1, oh2), (os0, os1, os2)
    cfs, scs, oms, sents = (cf0, cf1, cf2), (sc0, sc1, sc2), (om0, om1, om2), (sent0, sent1, sent2)
    prods, stacks, xjs = (prod0, prod1, prod2), (stack0, stack1, stack2), (xj0, xj1, xj2)
    xis, turn_of = (xi0, xi1, xi2), (tn0, tn1, tn2)
    xxs, xms, xss = (xx0, xx1, xx2), (xm0, xm1, xm2), (xs0, xs1, xs2)
    total = n_dom * N_SUB
    dom = lax.axis_index("dom")
    sub = lax.axis_index("sub")
    me = dom * N_SUB + sub
    up = (me + 1) % total
    down = (me + total - 1) % total
    up_id = (up // N_SUB, up % N_SUB)
    down_id = (down // N_SUB, down % N_SUB)
    first, last = me == 0, me == total - 1

    barrier = pltpu.get_barrier_semaphore()

    @pl.when(jnp.logical_not(last))
    def _():
        pl.semaphore_signal(barrier, inc=1, device_id=up_id, device_id_type=MESH)

    @pl.when(jnp.logical_not(first))
    def _():
        pl.semaphore_signal(barrier, inc=1, device_id=down_id, device_id_type=MESH)

    for k in range(1, N_SUB):
        pl.semaphore_signal(
            barrier, inc=1, device_id=(dom, (sub + k) % N_SUB), device_id_type=MESH
        )

    def halo_copies(send, recv, ssem, rsem, slot):
        return [
            pltpu.make_async_remote_copy(
                src_ref=send.at[slot, way], dst_ref=recv.at[slot, way],
                send_sem=ssem.at[slot, way], recv_sem=rsem.at[slot, way],
                device_id=(up_id, down_id)[way], device_id_type=MESH,
            )
            for way in range(2)
        ]

    def group_copies(send, recv, number):
        found = []
        for k in range(1, N_SUB):
            dest = (sub + k) % N_SUB
            found.append(
                pltpu.make_async_remote_copy(
                    src_ref=send.at[dest], dst_ref=recv.at[sub],
                    send_sem=gss.at[number, k], recv_sem=grs.at[number, k],
                    device_id=(dom, dest), device_id_type=MESH,
                )
            )
        return found

    held = (wave, mat, geo, fs, der, lift, nbr, ori, halo, iface, place, select, spread, turns)
    fetch = {
        i: pltpu.make_async_copy(ins[i], held[i], in_sems.at[i])
        for i in (4, 5, 10, 11, 12, 0, 8, 9, 1, 2, 3, 7, 6, 13)
    }
    for copy in fetch.values():
        copy.start()

    def fetched(*numbers):
        for i in numbers:
            fetch[i].wait()

    for end, way in ((first, 0), (last, 1)):

        @pl.when(end)
        def _():
            for ref in (hr0, hr1, hr2):
                ref[:, way] = jnp.zeros((ref.shape[0],) + ref.shape[2:], F32)

    halo_f = [halo_copies(hs0, hr0, ss0, rs0, s) for s in range(4)]
    halo_m = [halo_copies(hs1, hr1, ss1, rs1, s) for s in range(2)]
    halo_c = halo_copies(hs2, hr2, ss2, rs2, 0)
    group = [
        group_copies(s, r, i)
        for i, (s, r) in enumerate(((gs0, gr0), (gs1, gr1), (gs2, gr2), (gs3, gr3), (gs4, gr4)))
    ]

    dpad[...] = jnp.zeros_like(dpad)
    lpad[...] = jnp.zeros_like(lpad)
    fetched(4, 5, 10, 11, 12)
    for k in range(3):
        dpad[k, 0:35, 0:35] = der[k]
    lpad[0:35, 0:60] = lift[...]
    parts = []
    for k in range(3):
        high, low = split(dpad[k])
        parts.append(dot(high, place[0]) + dot(low, place[1]))
    amat[...] = jnp.concatenate(parts, axis=0).astype(BF16)
    smat[...] = select[:, 0:96].astype(BF16)
    emat[...] = (select[0:64, 0:96] + select[64:128, 0:96]).astype(BF16)
    high, low = split(lpad[...])
    lmat[0:48] = dot(high, spread[0]).astype(BF16)
    lmat[48:96] = dot(low, spread[1]).astype(BF16)

    def remap(index, c):
        if c:
            return index
        return jnp.where(
            index < 256, (index & 63) + ((index >> 6) << 7), index + 256
        )

    def order_of(turned):
        return jnp.where(turned == 0, turns[0], jnp.where(turned == 1, turns[1], turns[2]))

    def reorder(x, order):
        found = []
        for half in (order[0:8], order[8:16]):
            row = half & 7
            low = jnp.take_along_axis(x[0:8], row, axis=0, mode="promise_in_bounds")
            high = jnp.take_along_axis(x[8:16], row, axis=0, mode="promise_in_bounds")
            found.append(jnp.where(half < 8, low, high))
        return jnp.concatenate(found, axis=0)

    def load(c):
        first, wide = LANE[c], WIDE[c]
        span = slice(first, first + wide)
        u = us[c]
        for q in range(9):
            u[q, 32:40, :] = jnp.zeros((8, wide), F32)
            u[q, 0:35, :] = wave[q, :, span]

    def coefficients(c):
        first, wide = LANE[c], WIDE[c]
        span = slice(first, first + wide)
        rho = STEP[c] / mat[0:1, span]
        lam = STEP[c] * mat[1:2, span]
        mu = STEP[c] * mat[2:3, span]
        cf = cfs[c]
        for i in range(3):
            axes = geo[i, :, span]
            cf[3 * i : 3 * i + 3] = axes * mu
            cf[9 + 3 * i : 12 + 3 * i] = axes * rho
            cf[18 + 3 * i : 21 + 3 * i] = axes
        cf[27:28] = lam
        cf[28:29] = 2.0 * mu
        for f in range(4):
            where = slice(f * wide, (f + 1) * wide)
            scs[c][:, where] = (0.5 * STEP[c]) * fs[f : f + 1, span]
            turn_of[c][f : f + 1] = ori[f : f + 1, span]
            for j in range(wide // 128):
                oms[c][f * wide // 128 + j] = order_of(
                    jnp.broadcast_to(turn_of[c][f : f + 1, 128 * j : 128 * j + 128], (16, 128))
                )

    def send_table(c):
        blank = jnp.full((1, 64), -1, jnp.int32)
        if c == 0:
            rows = [(halo[0:1, 0:32], halo[1:2, 0:32], iface[0, 0:1], iface[1, 0:1])]
        elif c == 1:
            rows = [(halo[0:1, 32:96], halo[1:2, 32:96]), (iface[0, 1:2], iface[2, 0:1], blank)]
        else:
            rows = [(halo[0:1, 96:224],), (halo[1:2, 96:224],)]
        for i, row in enumerate(rows):
            at = slice(3 * c + i, 3 * c + i + 1)
            row_of[at] = remap(jnp.concatenate(row, axis=1), c)
            fill_one_hot(oss[c], i, [row_of[at]])

    def neighbour_table(c):
        wide, own, ext = WIDE[c], OWN[c], EXT[c]
        span = slice(LANE[c], LANE[c] + wide)
        index = remap(nbr[:, span], c)
        if c == 0:
            index = jnp.where(lanes(index.shape) < 64, index, -1)
        ixs = (ix0, ix1, ix2)[c]
        ixs[...] = jnp.full((8, wide), -1, jnp.int32)
        ixs[0:4] = index
        upright = (ixs[...] - own).astype(F32).T
        across = lanes((32, ext)).astype(F32)
        scale_at, turned_at = None, None
        for f in range(4):
            face = slice(f * wide, (f + 1) * wide)
            fill_one_hot(ohs[c], f * wide // 128, [ixs[f : f + 1]])
            high, low = split(jnp.broadcast_to(scs[c][:, face], (16, wide)))
            turned = jnp.broadcast_to(turn_of[c][f : f + 1].astype(F32), (16, wide)).astype(BF16)
            tall = jnp.concatenate([turned, jnp.ones((16, wide), BF16), high, low], axis=0)
            for start in range(0, wide, 32):
                column = jnp.broadcast_to(upright[start : start + 32, f : f + 1], (32, ext))
                put(xtab, slice(start, start + 32), 0, jnp.where(column == across, 1.0, 0.0).astype(BF16))
            found = dot(tall, get(xtab, slice(0, wide), 0, ext // 128))
            put(xms[c].at[f], slice(None), 0, found[16:32].astype(BF16))
            both = found[32:48] + found[48:64]
            scale_at = both if scale_at is None else scale_at + both
            turned_at = found[0:16] if turned_at is None else turned_at + found[0:16]
        for i in range(ext // 128):
            xis[c][i] = order_of(turned_at[:, 128 * i : 128 * i + 128].astype(jnp.int32))
        fill_one_hot(xxs[c], 0, [ixs[f : f + 1] for f in range(4)], own)
        xss[c][...] = scale_at

    def early(c, row):
        wide = WIDE[c]
        at = slice(2 * c - 1, 2 * c)
        row_of[at] = row
        row = row_of[at]
        element, face = row & (wide - 1), row >> (7 if c == 1 else 8)
        tall = jnp.concatenate([us[c][q] for q in range(9)], axis=0)
        high = tall.astype(BF16).astype(F32)
        both = jnp.concatenate([high, tall - high], axis=0).astype(BF16)
        fill_one_hot(xtab, 0, [element], rows=wide)
        picked = dot(both, xtab[0, 0:wide])
        gap = jnp.zeros((8, 128), F32)
        for q in range(9):
            pair = [picked[40 * q : 40 * q + 40], gap, picked[360 + 40 * q : 400 + 40 * q], gap]
            stack3[q] = jnp.concatenate(pair, axis=0).astype(BF16)
        nodes = dot(emat[...], get(stack3))
        face = jnp.broadcast_to(face, (16, 128))
        found = []
        for q in range(9):
            span = slice(128 * q, 128 * q + 128)
            acc = jnp.zeros((16, 128), F32)
            for f in range(4):
                acc = jnp.where(face == f, nodes[16 * f : 16 * f + 16, span], acc)
            found.append(acc)
        return jnp.concatenate(found, axis=0)

    def traces(c):
        wide = WIDE[c]
        u, t, stack = us[c], ts[c], stacks[c]
        gap = jnp.zeros((8, wide), F32)
        for q in range(9):
            x = u[q]
            high = x.astype(BF16).astype(F32)
            tall = jnp.concatenate([high, gap, x - high, gap, high, gap], axis=0)
            put(stack, slice(None), q * wide // 128, tall.astype(BF16))
        picked = dot(smat[...], get(stack, slice(0, 96)))
        for q in range(9):
            where = slice(q * wide, (q + 1) * wide)
            for part in range(2):
                for f in range(4):
                    row = 64 * part + 16 * f
                    at = 144 * part + 16 * q
                    value = picked[row : row + 16, where].astype(BF16)
                    put(t, slice(at, at + 16), f * wide // 128, value)
        both = dot(get(t), get(oss[c]))
        sents[c][...] = both[0:144] + both[144:288]

    def volume(c):
        wide = WIDE[c]
        cf, prod, t = cfs[c], prods[c], ts[c]
        tiles, own_tiles = wide // 128, OWN[c] // 128
        prod[...] = dot(amat[...], get(stacks[c]))
        both = dot(get(t), get(ohs[c]))
        gs_[c][...] = both[0:144] + both[144:288]
        scale = scs[c][...]
        for j in range(own_tiles):
            lane = slice(128 * j, 128 * j + 128)
            f, part = j // tiles, j % tiles
            order = oms[c][j]
            for q in range(9):
                at = 16 * q
                outer = reorder(gs_[c][at : at + 16, lane], order)
                mine = t[j, at : at + 16].astype(F32) + t[j, 144 + at : 160 + at].astype(F32)
                high, low = split((outer - mine) * scale[:, lane])
                jump[q * tiles + part, 16 * f : 16 * f + 16] = high
                jump[q * tiles + part, 64 + 16 * f : 80 + 16 * f] = low
        first = dot(lmat[...], get(jump, slice(None), 0, 9 * tiles))
        whole = first[0:40] + first[48:88]
        for start in range(0, wide, 128):
            span = slice(start, start + 128)

            def old(q):
                at = q * wide + start
                return us[c][q, :, span] + whole[:, at : at + 128]

            def grad(q, i, kind):
                at = q * wide + start
                base = 9 * kind + 3 * i
                return sum(
                    jnp.broadcast_to(cf[base + k : base + k + 1, span], (40, 128))
                    * prod[40 * k : 40 * k + 40, at : at + 128]
                    for k in range(3)
                )

            for i in range(3):
                rate = grad(VOIGT[i][0], 0, 1) + grad(VOIGT[i][1], 1, 1) + grad(VOIGT[i][2], 2, 1)
                vs[c][i, :, span] = old(i) + rate
            diag = [grad(i, i, 2) for i in range(3)]
            shared = cf[27:28, span] * (diag[0] + diag[1] + diag[2])
            for i in range(3):
                vs[c][3 + i, :, span] = old(3 + i) + (shared + cf[28:29, span] * diag[i])
            for q, i, j in ((6, 1, 2), (7, 0, 2), (8, 0, 1)):
                rate = grad(j, i, 0) + grad(i, j, 0)
                vs[c][q, :, span] = old(q) + rate

    def receive(c, tile, value, new=False):
        span = slice(128 * tile, 128 * tile + 128)
        xj = xjs[c]
        scale, order = xss[c][:, span], xis[c][tile]
        for q in range(9):
            high, low = split(reorder(value[16 * q : 16 * q + 16], order) * scale)
            for f in range(4):
                mask = xms[c][f, tile]
                xj[q, 16 * f : 16 * f + 16] = high * mask
                xj[q, 64 + 16 * f : 80 + 16 * f] = low * mask
        first = dot(lmat[...], get(xj))
        whole = first[0:40] + first[48:88]
        tall = jnp.concatenate([whole[:, 128 * q : 128 * q + 128] for q in range(9)], axis=0)
        high = tall.astype(BF16).astype(F32)
        both = jnp.concatenate([high, tall - high], axis=0).astype(BF16)
        added = dot(both, get(xxs[c], span))
        target = us[c] if new else vs[c]
        for q in range(9):
            at = 40 * q
            target[q] = vs[c][q] + (added[at : at + 40] + added[360 + at : 400 + at])

    lane48 = lanes((48, 128))
    lane16 = lanes((16, 128))

    def pack_third(x, base):
        return jnp.where(
            lane48 < 32, turn(x[0:48], -base),
            jnp.where(lane48 < 64, turn(x[48:96], 32 - base), turn(x[96:144], 64 - base)),
        )

    def send_fine(slot):
        x = sent0[...]
        hs0[slot, 0] = pack_third(x, 32)
        hs0[slot, 1] = pack_third(x, 0)

    def send_middle(slot):
        x = sent1[:, 0:128]
        lower = x[0:80]
        upper = jnp.concatenate([x[80:144], jnp.zeros((16, 128), F32)], axis=0)
        left = lanes((80, 128)) < 64
        hs1[slot, 0] = jnp.where(left, turn(lower, 64), upper)
        hs1[slot, 1] = jnp.where(left, lower, turn(upper, 64))

    def send_group(send, recv, number, x, base):
        rows = slice(16 * number, 16 * number + 16)
        for j in range(N_SUB):
            acc = jnp.zeros((16, 128), F32)
            for q in range(9):
                piece = turn(x[16 * q : 16 * q + 16], 8 * q - base - 8 * j)
                acc = jnp.where((lane16 >= 8 * q) & (lane16 < 8 * q + 8), piece, acc)
            send[j, rows] = acc
        recv[sub, rows] = send[sub, rows]

    def take_group(recv, number, base):
        rows = slice(16 * number, 16 * number + 16)
        pieces = [recv[p, rows] for p in range(N_SUB)]
        found = []
        for q in range(9):
            acc = jnp.zeros((16, 128), F32)
            for p in range(N_SUB):
                at = base + 8 * p
                acc = jnp.where(
                    (lane16 >= at) & (lane16 < at + 8), turn(pieces[p], at - 8 * q), acc
                )
            found.append(acc)
        return jnp.concatenate(found, axis=0)

    def start(copies):
        for copy in copies:
            copy.start()

    def arrive(copies):
        for copy in copies:
            copy.wait_recv()

    def start_halo(copies):
        pl.when(jnp.logical_not(last))(copies[0].start)
        pl.when(jnp.logical_not(first))(copies[1].start)

    def arrive_halo(copies):
        pl.when(jnp.logical_not(first))(copies[0].wait_recv)
        pl.when(jnp.logical_not(last))(copies[1].wait_recv)

    def fine_halo(slot):
        below = hr0[slot, 0]
        above = hr0[slot, 1]
        found = []
        for r in range(3):
            found.append(
                jnp.where(
                    lane48 < 32, turn(below, -32 * r),
                    jnp.where(lane48 < 64, turn(above, 32 - 32 * r), base0[48 * r : 48 * r + 48]),
                )
            )
        receive(0, 0, jnp.concatenate(found, axis=0), new=True)

    def middle_halo(slot):
        below = hr1[slot, 0]
        above = hr1[slot, 1]
        left = lanes((80, 128)) < 64
        lower = jnp.where(left, below, turn(above, 64))
        upper = jnp.where(left, turn(below, 64), above)
        receive(1, 0, jnp.concatenate([lower, upper[0:64]], axis=0))

    fetched(0, 8, 9)
    load(0)
    send_table(0)
    traces(0)
    sum_a[...] = sent0[...]
    send_fine(0)
    pl.semaphore_wait(barrier, N_SUB - 1 + (me + total - 1) // total + 1 - (me + 1) // total)
    start_halo(halo_f[0])
    load(1)
    load(2)
    blank = jnp.full((1, 64), -1, jnp.int32)
    start_m = early(1, jnp.concatenate([iface[0, 1:2], iface[2, 0:1], blank], axis=1))
    start_c = early(2, jnp.concatenate([iface[1, 1:2], iface[2, 1:2], blank], axis=1))
    sum_b[...] = start_m
    send_group(gs0, gr0, 0, start_m, 0)
    send_group(gs0, gr0, 1, start_c, 0)
    start(group[0])
    send_group(gs4, gr4, 0, start_c, 32)
    start(group[4])
    send_table(1)
    traces(1)
    send_middle(0)
    start_halo(halo_m[0])
    send_table(2)
    traces(2)
    hs2[0, 0] = sent2[:, 128:256]
    hs2[0, 1] = sent2[:, 0:128]
    start_halo(halo_c)
    fetched(1, 2, 3, 7, 6, 13)
    coefficients(0)
    neighbour_table(0)
    volume(0)
    coefficients(1)
    coefficients(2)
    neighbour_table(1)
    arrive(group[0])
    base0[...] = take_group(gr0, 0, 64) + take_group(gr0, 1, 96)

    arrive_halo(halo_f[0])
    fine_halo(0)
    traces(0)
    send_fine(1)
    start_halo(halo_f[1])
    sum_a[...] += sent0[...]
    send_group(gs1, gr1, 0, 0.5 * sum_a[...], 64)
    start(group[1])
    volume(0)
    volume(1)
    arrive_halo(halo_m[0])
    middle_halo(0)
    arrive(group[4])
    start_mc = take_group(gr4, 0, 32)
    neighbour_table(2)

    arrive_halo(halo_f[1])
    fine_halo(1)
    traces(0)
    send_fine(2)
    start_halo(halo_f[2])
    sum_a[...] = 0.25 * sum_a[...] + 0.25 * sent0[...]
    base1 = sent0[...]
    volume(0)

    arrive(group[1])
    receive(1, 1, take_group(gr1, 0, 0) + start_mc, new=True)
    traces(1)
    send_middle(1)
    start_halo(halo_m[1])
    send_group(gs2, gr2, 0, 0.5 * (sum_b[...] + sent1[:, 128:256]), 32)
    start(group[2])
    volume(2)

    arrive_halo(halo_f[2])
    fine_halo(2)
    traces(0)
    send_fine(3)
    start_halo(halo_f[3])
    sum_a[...] += 0.25 * sent0[...]
    send_group(gs3, gr3, 0, 0.5 * (base1 + sent0[...]), 64)
    send_group(gs3, gr3, 1, sum_a[...], 96)
    start(group[3])
    volume(0)
    volume(1)
    arrive_halo(halo_m[1])
    middle_halo(1)
    arrive_halo(halo_c)
    receive(2, 0, hr2[0, 0])
    receive(2, 1, hr2[0, 1])
    arrive(group[2])
    mean = take_group(gr2, 0, 32)

    arrive_halo(halo_f[3])
    arrive(group[3])
    fine_halo(3)
    receive(1, 1, take_group(gr3, 0, 0) + start_mc, new=True)
    receive(2, 2, take_group(gr3, 1, 0) + mean, new=True)
    for q in range(9):
        out[q, :, 0:64] = u0[q, 0:35, 0:64]
        out[q, :, 64:192] = u1[q, 0:35, :]
        out[q, :, 192:448] = u2[q, 0:35, :]
    for copies in halo_f + halo_m + [halo_c]:
        pl.when(jnp.logical_not(last))(copies[0].wait_send)
        pl.when(jnp.logical_not(first))(copies[1].wait_send)
    for copies in group:
        for copy in copies:
            copy.wait_send()


def scratch(held):
    shapes = [pltpu.VMEM(x.shape, x.dtype) for x in held]
    shapes += [pltpu.SemaphoreType.DMA((len(held),))]
    shapes += [pltpu.VMEM((9, 40, w), F32) for w in WIDE] * 2
    shapes += [pltpu.VMEM((o // 128, 288, 128), BF16) for o in OWN]
    shapes += [pltpu.VMEM((144, o), F32) for o in OWN]
    shapes += [pltpu.VMEM((9 * w // 128, 144, 128), BF16) for w in WIDE]
    shapes += [pltpu.VMEM((9, 96, 128), BF16)]
    shapes += [pltpu.VMEM((120, 9 * w), F32) for w in WIDE]
    shapes += [pltpu.VMEM((18, 128, 128), BF16)]
    shapes += [pltpu.VMEM((9, 128, 128), BF16)] * 3
    shapes += [pltpu.VMEM((o // 128, o, 128), BF16) for o in OWN]
    shapes += [pltpu.VMEM((w // 128, e, 128), BF16) for e, w in zip(EXT, WIDE)]
    shapes += [pltpu.VMEM((4, e // 128, 16, 128), BF16) for e in EXT]
    shapes += [pltpu.VMEM((16, e), F32) for e in EXT]
    shapes += [pltpu.VMEM((e // 128, 16, 128), jnp.int32) for e in EXT]
    shapes += [pltpu.VMEM((8, w), jnp.int32) for w in WIDE]
    shapes += [pltpu.VMEM((s // 128, o, 128), BF16) for o, s in zip(OWN, SENT)]
    shapes += [pltpu.VMEM((32, w), F32) for w in WIDE]
    shapes += [pltpu.VMEM((1, o), F32) for o in OWN]
    shapes += [pltpu.VMEM((o // 128, 16, 128), jnp.int32) for o in OWN]
    shapes += [pltpu.VMEM((8, w), jnp.int32) for w in WIDE] + [pltpu.VMEM((8, 128), jnp.int32)]
    shapes += [pltpu.VMEM((3, 256, 128), BF16)]
    shapes += [pltpu.VMEM((3, 40, 128), F32), pltpu.VMEM((48, 128), F32)]
    shapes += [pltpu.VMEM((120, 144), BF16), pltpu.VMEM((128, 96), BF16)]
    shapes += [pltpu.VMEM((64, 96), BF16), pltpu.VMEM((96, 128), BF16)]
    shapes += [pltpu.VMEM((144, s), F32) for s in SENT]
    shapes += [pltpu.VMEM((144, 128), F32)] * 3
    shapes += [pltpu.VMEM((4, 2, 48, 128), F32)] * 2
    shapes += [pltpu.VMEM((2, 2, 80, 128), F32)] * 2
    shapes += [pltpu.VMEM((1, 2, 144, 128), F32)] * 2
    for buffers in (2, 1, 1, 2, 1):
        shapes += [pltpu.VMEM((N_SUB, 16 * buffers, 128), F32)] * 2
    for slots in (4, 2, 1):
        shapes += [pltpu.SemaphoreType.DMA((slots, 2))] * 2
    shapes += [pltpu.SemaphoreType.DMA((5, 4))] * 2
    return shapes


def solution(mesh):
    n_dom = mesh.shape["dom"]
    place, select, spread, turns = constants()

    def on_device(*arrays):
        held = arrays[:-1] + (
            arrays[-1].transpose(1, 0, 2),
            jnp.asarray(place, BF16), jnp.asarray(select, F32), jnp.asarray(spread, BF16),
            jnp.asarray(turns),
        )
        return pl.pallas_call(
            functools.partial(kernel, n_dom),
            out_shape=pltpu.VMEM(arrays[0].shape, F32),
            in_specs=[pl.BlockSpec(memory_space=pltpu.HBM)] * 14,
            out_specs=pl.BlockSpec(memory_space=pltpu.VMEM),
            scratch_shapes=scratch(held),
            compiler_params=pltpu.CompilerParams(
                collective_id=0, has_side_effects=True, vmem_limit_bytes=60 * 1024 * 1024
            ),
            name="step",
        )(*held)

    split_all = ("dom", "sub")
    placed = (
        P(None, None, split_all), P(None, split_all), P(None, None, split_all),
        P(None, split_all), P(), P(), P(None, split_all), P(None, split_all),
        P(None, split_all), P(None, None, split_all),
    )
    return jax.shard_map(
        on_device, mesh=mesh, in_specs=placed, out_specs=P(None, None, split_all), check_vma=False,
    )
```

```python
import functools

import jax
import jax.numpy as jnp
import numpy as np
from jax import lax
from jax.experimental import pallas as pl
from jax.experimental.pallas import tpu as pltpu
from jax.sharding import PartitionSpec as P

F32 = jnp.float32
BF16 = jnp.bfloat16
MESH = pl.DeviceIdType.MESH
N_SUB = 4
COARSE_STEP = 0.1

LANE = (0, 64, 192)
WIDE = (128, 128, 256)
OWN = (512, 512, 1024)
EXT = (128, 256, 384)
SENT = (128, 256, 256)
STEP = (COARSE_STEP / 4, COARSE_STEP / 2, COARSE_STEP)

VOIGT = ((3, 8, 7), (8, 4, 6), (7, 6, 5))


def face_tables():
    lattice = [
        (a, b, c, 4 - a - b - c) for a in range(5) for b in range(5 - a) for c in range(5 - a - b)
    ]
    face_rows = np.array(
        [[i for i, p in enumerate(lattice) if p[f] == 0] for f in range(4)], np.int32
    )
    triangle = [p[1:] for p in lattice if p[0] == 0]
    position = {p: i for i, p in enumerate(triangle)}

    def turned(p, times):
        p = (p[1], p[0], p[2])
        for _ in range(times):
            p = (p[1], p[2], p[0])
        return p

    orders = np.array(
        [[position[turned(p, o)] for p in triangle] for o in range(3)], np.int32
    )
    return face_rows, orders


def constants():
    face_rows, orders = face_tables()
    place = np.zeros((2, 128, 144), np.float32)
    for n in range(35):
        place[0, n, n] = 1
        place[0, n, 48 + n] = 1
        place[1, n, 96 + n] = 1
    select = np.zeros((128, 144), np.float32)
    for f in range(4):
        for n in range(15):
            select[f * 16 + n, face_rows[f, n]] = 1
            select[64 + f * 16 + n, 48 + face_rows[f, n]] = 1
    spread = np.zeros((2, 128, 128), np.float32)
    for f in range(4):
        for n in range(15):
            spread[0, f * 15 + n, f * 16 + n] = 1
            spread[0, f * 15 + n, 64 + f * 16 + n] = 1
            spread[1, f * 15 + n, f * 16 + n] = 1
    turns = np.full((3, 16, 128), 15, np.int32)
    turns[:, :15] = orders[:, :, None]
    return place, select, spread, turns


def split(x):
    high = x.astype(BF16)
    return high, (x - high.astype(F32)).astype(BF16)


def dot(a, b):
    return jnp.dot(a, b, preferred_element_type=F32)


def lanes(shape):
    return lax.broadcasted_iota(jnp.int32, shape, 1)


def turn(x, shift):
    shift %= 128
    return pltpu.roll(x, shift, 1) if shift else x


def put(ref, rows, tile, value):
    for i in range(value.shape[1] // 128):
        ref[tile + i, rows, :] = value[:, 128 * i : 128 * i + 128]


def get(ref, rows=slice(None), start=0, stop=None):
    stop = ref.shape[0] if stop is None else stop
    return jnp.concatenate([ref[i, rows, :] for i in range(start, stop)], axis=1)


def fill_one_hot(ref, tile, indices, base=0, rows=None):
    chunk = 32
    for start in range(0, rows or ref.shape[1], chunk):
        iota = lax.broadcasted_iota(jnp.int32, (chunk, indices[0].shape[1]), 0)
        hit = None
        for index in indices:
            here = iota == jnp.broadcast_to(index - (base + start), iota.shape)
            hit = here if hit is None else hit | here
        put(ref, slice(start, start + chunk), tile, jnp.where(hit, 1.0, 0.0).astype(BF16))


def kernel(
    n_dom,
    *refs,
):
    ins, out, held, in_sems, rest = refs[:14], refs[14], refs[15:29], refs[29], refs[30:]
    body(n_dom, ins, in_sems, out, *held, *rest)


def body(
    n_dom, ins, in_sems, out,
    wave, mat, geo, fs, der, lift, nbr, ori, halo, iface, place, select, spread, turns,
    u0, u1, u2, v0, v1, v2, t0, t1, t2, g0, g1, g2,
    stack0, stack1, stack2, stack3, prod0, prod1, prod2, jump, xj0, xj1, xj2,
    oh0, oh1, oh2, xx0, xx1, xx2, xm0, xm1, xm2, xs0, xs1, xs2,
    xi0, xi1, xi2, tn0, tn1, tn2,
    os0, os1, os2, cf0, cf1, cf2, sc0, sc1, sc2, om0, om1, om2,
    ix0, ix1, ix2, row_of, xtab, dpad, lpad, amat, emat, lmat, sent0, sent1, sent2, sum_a, sum_b, base0,
    hs0, hr0, hs1, hr1, hs2, hr2, gs0, gr0, gs1, gr1, gs2, gr2, gs3, gr3, gs4, gr4,
    ss0, rs0, ss1, rs1, ss2, rs2, gss, grs,
):
    us, vs, ts, gs_, ohs, oss = (u0, u1, u2), (v0, v1, v2), (t0, t1, t2), (g0, g1, g2), (oh0, oh1, oh2), (os0, os1, os2)
    cfs, scs, oms, sents = (cf0, cf1, cf2), (sc0, sc1, sc2), (om0, om1, om2), (sent0, sent1, sent2)
    prods, stacks, xjs = (prod0, prod1, prod2), (stack0, stack1, stack2), (xj0, xj1, xj2)
    xis, turn_of = (xi0, xi1, xi2), (tn0, tn1, tn2)
    xxs, xms, xss = (xx0, xx1, xx2), (xm0, xm1, xm2), (xs0, xs1, xs2)
    total = n_dom * N_SUB
    dom = lax.axis_index("dom")
    sub = lax.axis_index("sub")
    me = dom * N_SUB + sub
    up = (me + 1) % total
    down = (me + total - 1) % total
    up_id = (up // N_SUB, up % N_SUB)
    down_id = (down // N_SUB, down % N_SUB)
    first, last = me == 0, me == total - 1

    barrier = pltpu.get_barrier_semaphore()

    @pl.when(jnp.logical_not(last))
    def _():
        pl.semaphore_signal(barrier, inc=1, device_id=up_id, device_id_type=MESH)

    @pl.when(jnp.logical_not(first))
    def _():
        pl.semaphore_signal(barrier, inc=1, device_id=down_id, device_id_type=MESH)

    for k in range(1, N_SUB):
        pl.semaphore_signal(
            barrier, inc=1, device_id=(dom, (sub + k) % N_SUB), device_id_type=MESH
        )

    def halo_copies(send, recv, ssem, rsem, slot):
        return [
            pltpu.make_async_remote_copy(
                src_ref=send.at[slot, way], dst_ref=recv.at[slot, way],
                send_sem=ssem.at[slot, way], recv_sem=rsem.at[slot, way],
                device_id=(up_id, down_id)[way], device_id_type=MESH,
            )
            for way in range(2)
        ]

    def group_copies(send, recv, number):
        found = []
        for k in range(1, N_SUB):
            dest = (sub + k) % N_SUB
            found.append(
                pltpu.make_async_remote_copy(
                    src_ref=send.at[dest], dst_ref=recv.at[sub],
                    send_sem=gss.at[number, k], recv_sem=grs.at[number, k],
                    device_id=(dom, dest), device_id_type=MESH,
                )
            )
        return found

    held = (wave, mat, geo, fs, der, lift, nbr, ori, halo, iface, place, select, spread, turns)
    fetch = {
        i: pltpu.make_async_copy(ins[i], held[i], in_sems.at[i])
        for i in (4, 5, 10, 11, 12, 0, 8, 9, 1, 2, 3, 7, 6, 13)
    }
    for copy in fetch.values():
        copy.start()

    def fetched(*numbers):
        for i in numbers:
            fetch[i].wait()

    for end, way in ((first, 0), (last, 1)):

        @pl.when(end)
        def _():
            for ref in (hr0, hr1, hr2):
                ref[:, way] = jnp.zeros((ref.shape[0],) + ref.shape[2:], F32)

    halo_f = [halo_copies(hs0, hr0, ss0, rs0, s) for s in range(4)]
    halo_m = [halo_copies(hs1, hr1, ss1, rs1, s) for s in range(2)]
    halo_c = halo_copies(hs2, hr2, ss2, rs2, 0)
    group = [
        group_copies(s, r, i)
        for i, (s, r) in enumerate(((gs0, gr0), (gs1, gr1), (gs2, gr2), (gs3, gr3), (gs4, gr4)))
    ]

    dpad[...] = jnp.zeros_like(dpad)
    lpad[...] = jnp.zeros_like(lpad)
    fetched(4, 5, 10, 11, 12)
    for k in range(3):
        dpad[k, 0:35, 0:35] = der[k]
    lpad[0:35, 0:60] = lift[...]
    parts = []
    for k in range(3):
        high, low = split(dpad[k])
        parts.append(dot(high, place[0]) + dot(low, place[1]))
    amat[...] = jnp.concatenate(parts, axis=0).astype(BF16)
    emat[...] = (select[0:64, 0:96] + select[64:128, 0:96]).astype(BF16)
    high, low = split(lpad[...])
    lmat[0:48] = dot(high, spread[0]).astype(BF16)
    lmat[48:96] = dot(low, spread[1]).astype(BF16)

    def remap(index, c):
        if c:
            return index
        return jnp.where(
            index < 256, (index & 63) + ((index >> 6) << 7), index + 256
        )

    def order_of(turned):
        return jnp.where(turned == 0, turns[0], jnp.where(turned == 1, turns[1], turns[2]))

    def reorder(x, order):
        found = []
        for half in (order[0:8], order[8:16]):
            row = half & 7
            low = jnp.take_along_axis(x[0:8], row, axis=0, mode="promise_in_bounds")
            high = jnp.take_along_axis(x[8:16], row, axis=0, mode="promise_in_bounds")
            found.append(jnp.where(half < 8, low, high))
        return jnp.concatenate(found, axis=0)

    def load(c):
        first, wide = LANE[c], WIDE[c]
        span = slice(first, first + wide)
        u = us[c]
        for q in range(9):
            u[q, 32:40, :] = jnp.zeros((8, wide), F32)
            u[q, 0:35, :] = wave[q, :, span]

    def coefficients(c):
        first, wide = LANE[c], WIDE[c]
        span = slice(first, first + wide)
        rho = STEP[c] / mat[0:1, span]
        lam = STEP[c] * mat[1:2, span]
        mu = STEP[c] * mat[2:3, span]
        cf = cfs[c]
        for i in range(3):
            axes = geo[i, :, span]
            cf[3 * i : 3 * i + 3] = axes * mu
            cf[9 + 3 * i : 12 + 3 * i] = axes * rho
            cf[18 + 3 * i : 21 + 3 * i] = axes
        cf[27:28] = lam
        cf[28:29] = 2.0 * mu
        for f in range(4):
            where = slice(f * wide, (f + 1) * wide)
            scs[c][:, where] = (0.5 * STEP[c]) * fs[f : f + 1, span]
            turn_of[c][f : f + 1] = ori[f : f + 1, span]
            for j in range(wide // 128):
                oms[c][f * wide // 128 + j] = order_of(
                    jnp.broadcast_to(turn_of[c][f : f + 1, 128 * j : 128 * j + 128], (16, 128))
                )

    def send_table(c):
        blank = jnp.full((1, 64), -1, jnp.int32)
        if c == 0:
            rows = [(halo[0:1, 0:32], halo[1:2, 0:32], iface[0, 0:1], iface[1, 0:1])]
        elif c == 1:
            rows = [(halo[0:1, 32:96], halo[1:2, 32:96]), (iface[0, 1:2], iface[2, 0:1], blank)]
        else:
            rows = [(halo[0:1, 96:224],), (halo[1:2, 96:224],)]
        for i, row in enumerate(rows):
            at = slice(3 * c + i, 3 * c + i + 1)
            row_of[at] = remap(jnp.concatenate(row, axis=1), c)
            fill_one_hot(oss[c], i, [row_of[at]])

    def neighbour_table(c):
        wide, own = WIDE[c], OWN[c]
        span = slice(LANE[c], LANE[c] + wide)
        index = remap(nbr[:, span], c)
        if c == 0:
            index = jnp.where(lanes(index.shape) < 64, index, -1)
        ixs = (ix0, ix1, ix2)[c]
        ixs[...] = jnp.full((8, wide), -1, jnp.int32)
        ixs[0:4] = index
        for f in range(4):
            fill_one_hot(ohs[c], f * wide // 128, [ixs[f : f + 1]])

    def received_table(c):
        wide, own, ext = WIDE[c], OWN[c], EXT[c]
        ixs = (ix0, ix1, ix2)[c]
        upright = (ixs[...] - own).astype(F32).T
        across = lanes((32, ext)).astype(F32)
        scale_at, turned_at = None, None
        for f in range(4):
            face = slice(f * wide, (f + 1) * wide)
            high, low = split(jnp.broadcast_to(scs[c][:, face], (16, wide)))
            turned = jnp.broadcast_to(turn_of[c][f : f + 1].astype(F32), (16, wide)).astype(BF16)
            tall = jnp.concatenate([turned, jnp.ones((16, wide), BF16), high, low], axis=0)
            for start in range(0, wide, 32):
                column = jnp.broadcast_to(upright[start : start + 32, f : f + 1], (32, ext))
                put(xtab, slice(start, start + 32), 0, jnp.where(column == across, 1.0, 0.0).astype(BF16))
            found = dot(tall, get(xtab, slice(0, wide), 0, ext // 128))
            put(xms[c].at[f], slice(None), 0, found[16:32].astype(BF16))
            both = found[32:48] + found[48:64]
            scale_at = both if scale_at is None else scale_at + both
            turned_at = found[0:16] if turned_at is None else turned_at + found[0:16]
        for i in range(ext // 128):
            xis[c][i] = order_of(turned_at[:, 128 * i : 128 * i + 128].astype(jnp.int32))
        fill_one_hot(xxs[c], 0, [ixs[f : f + 1] for f in range(4)], own)
        xss[c][...] = scale_at

    def early(c, row):
        wide = WIDE[c]
        at = slice(2 * c - 1, 2 * c)
        row_of[at] = row
        row = row_of[at]
        element, face = row & (wide - 1), row >> (7 if c == 1 else 8)
        tall = jnp.concatenate([us[c][q] for q in range(9)], axis=0)
        high = tall.astype(BF16).astype(F32)
        both = jnp.concatenate([high, tall - high], axis=0).astype(BF16)
        fill_one_hot(xtab, 0, [element], rows=wide)
        picked = dot(both, xtab[0, 0:wide])
        gap = jnp.zeros((8, 128), F32)
        for q in range(9):
            pair = [picked[40 * q : 40 * q + 40], gap, picked[360 + 40 * q : 400 + 40 * q], gap]
            stack3[q] = jnp.concatenate(pair, axis=0).astype(BF16)
        nodes = dot(emat[...], get(stack3))
        face = jnp.broadcast_to(face, (16, 128))
        found = []
        for q in range(9):
            span = slice(128 * q, 128 * q + 128)
            acc = jnp.zeros((16, 128), F32)
            for f in range(4):
                acc = jnp.where(face == f, nodes[16 * f : 16 * f + 16, span], acc)
            found.append(acc)
        return jnp.concatenate(found, axis=0)

    def traces(c):
        wide = WIDE[c]
        u, t, stack = us[c], ts[c], stacks[c]
        gap = jnp.zeros((8, wide), F32)
        for q in range(9):
            x = u[q]
            high = x.astype(BF16).astype(F32)
            tall = jnp.concatenate([high, gap, x - high, gap, high, gap], axis=0)
            put(stack, slice(None), q * wide // 128, tall.astype(BF16))
        picked = dot(emat[...], get(stack, slice(0, 96)))
        for q in range(9):
            where = slice(q * wide, (q + 1) * wide)
            for f in range(4):
                at, tile = 16 * q, f * wide // 128
                high, low = split(picked[16 * f : 16 * f + 16, where])
                put(t, slice(at, at + 16), tile, high)
                put(t, slice(144 + at, 160 + at), tile, low)
        both = dot(get(t), get(oss[c]))
        sents[c][...] = both[0:144] + both[144:288]

    def volume(c):
        wide = WIDE[c]
        cf, prod, t = cfs[c], prods[c], ts[c]
        tiles, own_tiles = wide // 128, OWN[c] // 128
        prod[...] = dot(amat[...], get(stacks[c]))
        both = dot(get(t), get(ohs[c]))
        gs_[c][...] = both[0:144] + both[144:288]
        scale = scs[c][...]
        for j in range(own_tiles):
            lane = slice(128 * j, 128 * j + 128)
            f, part = j // tiles, j % tiles
            order = oms[c][j]
            for q in range(9):
                at = 16 * q
                outer = reorder(gs_[c][at : at + 16, lane], order)
                mine = t[j, at : at + 16].astype(F32) + t[j, 144 + at : 160 + at].astype(F32)
                high, low = split((outer - mine) * scale[:, lane])
                jump[q * tiles + part, 16 * f : 16 * f + 16] = high
                jump[q * tiles + part, 64 + 16 * f : 80 + 16 * f] = low
        first = dot(lmat[...], get(jump, slice(None), 0, 9 * tiles))
        whole = first[0:40] + first[48:88]
        for start in range(0, wide, 128):
            span = slice(start, start + 128)

            def old(q):
                at = q * wide + start
                return us[c][q, :, span] + whole[:, at : at + 128]

            def grad(q, i, kind):
                at = q * wide + start
                base = 9 * kind + 3 * i
                return sum(
                    jnp.broadcast_to(cf[base + k : base + k + 1, span], (40, 128))
                    * prod[40 * k : 40 * k + 40, at : at + 128]
                    for k in range(3)
                )

            for i in range(3):
                rate = grad(VOIGT[i][0], 0, 1) + grad(VOIGT[i][1], 1, 1) + grad(VOIGT[i][2], 2, 1)
                vs[c][i, :, span] = old(i) + rate
            diag = [grad(i, i, 2) for i in range(3)]
            shared = cf[27:28, span] * (diag[0] + diag[1] + diag[2])
            for i in range(3):
                vs[c][3 + i, :, span] = old(3 + i) + (shared + cf[28:29, span] * diag[i])
            for q, i, j in ((6, 1, 2), (7, 0, 2), (8, 0, 1)):
                rate = grad(j, i, 0) + grad(i, j, 0)
                vs[c][q, :, span] = old(q) + rate

    def receive(c, tile, value, new=False):
        span = slice(128 * tile, 128 * tile + 128)
        xj = xjs[c]
        scale, order = xss[c][:, span], xis[c][tile]
        for q in range(9):
            high, low = split(reorder(value[16 * q : 16 * q + 16], order) * scale)
            for f in range(4):
                mask = xms[c][f, tile]
                xj[q, 16 * f : 16 * f + 16] = high * mask
                xj[q, 64 + 16 * f : 80 + 16 * f] = low * mask
        first = dot(lmat[...], get(xj))
        whole = first[0:40] + first[48:88]
        tall = jnp.concatenate([whole[:, 128 * q : 128 * q + 128] for q in range(9)], axis=0)
        high = tall.astype(BF16).astype(F32)
        both = jnp.concatenate([high, tall - high], axis=1).astype(BF16)
        columns = get(xxs[c], span)
        added = dot(both, jnp.concatenate([columns, columns], axis=0))
        target = us[c] if new else vs[c]
        for q in range(9):
            at = 40 * q
            target[q] = vs[c][q] + added[at : at + 40]

    lane48 = lanes((48, 128))
    lane16 = lanes((16, 128))

    def pack_third(x, base):
        return jnp.where(
            lane48 < 32, turn(x[0:48], -base),
            jnp.where(lane48 < 64, turn(x[48:96], 32 - base), turn(x[96:144], 64 - base)),
        )

    def send_fine(slot):
        x = sent0[...]
        hs0[slot, 0] = pack_third(x, 32)
        hs0[slot, 1] = pack_third(x, 0)

    def send_middle(slot):
        x = sent1[:, 0:128]
        lower = x[0:80]
        upper = jnp.concatenate([x[80:144], jnp.zeros((16, 128), F32)], axis=0)
        left = lanes((80, 128)) < 64
        hs1[slot, 0] = jnp.where(left, turn(lower, 64), upper)
        hs1[slot, 1] = jnp.where(left, lower, turn(upper, 64))

    def send_group(send, recv, number, x, base):
        rows = slice(16 * number, 16 * number + 16)
        for j in range(N_SUB):
            acc = jnp.zeros((16, 128), F32)
            for q in range(9):
                piece = turn(x[16 * q : 16 * q + 16], 8 * q - base - 8 * j)
                acc = jnp.where((lane16 >= 8 * q) & (lane16 < 8 * q + 8), piece, acc)
            send[j, rows] = acc
        recv[sub, rows] = send[sub, rows]

    def take_group(recv, number, base):
        rows = slice(16 * number, 16 * number + 16)
        pieces = [recv[p, rows] for p in range(N_SUB)]
        found = []
        for q in range(9):
            acc = jnp.zeros((16, 128), F32)
            for p in range(N_SUB):
                at = base + 8 * p
                acc = jnp.where(
                    (lane16 >= at) & (lane16 < at + 8), turn(pieces[p], at - 8 * q), acc
                )
            found.append(acc)
        return jnp.concatenate(found, axis=0)

    def start(copies):
        for copy in copies:
            copy.start()

    def arrive(copies):
        for copy in copies:
            copy.wait_recv()

    def start_halo(copies):
        pl.when(jnp.logical_not(last))(copies[0].start)
        pl.when(jnp.logical_not(first))(copies[1].start)

    def arrive_halo(copies):
        pl.when(jnp.logical_not(first))(copies[0].wait_recv)
        pl.when(jnp.logical_not(last))(copies[1].wait_recv)

    def fine_halo(slot):
        below = hr0[slot, 0]
        above = hr0[slot, 1]
        found = []
        for r in range(3):
            found.append(
                jnp.where(
                    lane48 < 32, turn(below, -32 * r),
                    jnp.where(lane48 < 64, turn(above, 32 - 32 * r), base0[48 * r : 48 * r + 48]),
                )
            )
        receive(0, 0, jnp.concatenate(found, axis=0), new=True)

    def middle_halo(slot):
        below = hr1[slot, 0]
        above = hr1[slot, 1]
        left = lanes((80, 128)) < 64
        lower = jnp.where(left, below, turn(above, 64))
        upper = jnp.where(left, turn(below, 64), above)
        receive(1, 0, jnp.concatenate([lower, upper[0:64]], axis=0))

    fetched(0, 8, 9)
    load(0)
    send_table(0)
    traces(0)
    sum_a[...] = sent0[...]
    send_fine(0)
    pl.semaphore_wait(barrier, N_SUB - 1 + (me + total - 1) // total + 1 - (me + 1) // total)
    start_halo(halo_f[0])
    load(1)
    load(2)
    blank = jnp.full((1, 64), -1, jnp.int32)
    start_m = early(1, jnp.concatenate([iface[0, 1:2], iface[2, 0:1], blank], axis=1))
    start_c = early(2, jnp.concatenate([iface[1, 1:2], iface[2, 1:2], blank], axis=1))
    sum_b[...] = start_m
    send_group(gs0, gr0, 0, start_m, 0)
    send_group(gs0, gr0, 1, start_c, 0)
    start(group[0])
    send_group(gs4, gr4, 0, start_c, 32)
    start(group[4])
    send_table(1)
    traces(1)
    send_middle(0)
    start_halo(halo_m[0])
    send_table(2)
    traces(2)
    hs2[0, 0] = sent2[:, 128:256]
    hs2[0, 1] = sent2[:, 0:128]
    start_halo(halo_c)
    fetched(1, 2, 3, 7, 6, 13)
    coefficients(0)
    neighbour_table(0)
    received_table(0)
    volume(0)
    coefficients(1)
    coefficients(2)
    neighbour_table(1)
    received_table(1)
    arrive(group[0])
    base0[...] = take_group(gr0, 0, 64) + take_group(gr0, 1, 96)

    arrive_halo(halo_f[0])
    fine_halo(0)
    traces(0)
    send_fine(1)
    start_halo(halo_f[1])
    sum_a[...] += sent0[...]
    send_group(gs1, gr1, 0, 0.5 * sum_a[...], 64)
    start(group[1])
    volume(0)
    volume(1)
    arrive_halo(halo_m[0])
    middle_halo(0)
    arrive(group[4])
    start_mc = take_group(gr4, 0, 32)
    neighbour_table(2)

    arrive_halo(halo_f[1])
    fine_halo(1)
    traces(0)
    send_fine(2)
    start_halo(halo_f[2])
    sum_a[...] = 0.25 * sum_a[...] + 0.25 * sent0[...]
    base1 = sent0[...]
    volume(0)

    arrive(group[1])
    receive(1, 1, take_group(gr1, 0, 0) + start_mc, new=True)
    traces(1)
    send_middle(1)
    start_halo(halo_m[1])
    send_group(gs2, gr2, 0, 0.5 * (sum_b[...] + sent1[:, 128:256]), 32)
    start(group[2])
    volume(2)

    arrive_halo(halo_f[2])
    fine_halo(2)
    traces(0)
    send_fine(3)
    start_halo(halo_f[3])
    sum_a[...] += 0.25 * sent0[...]
    send_group(gs3, gr3, 0, 0.5 * (base1 + sent0[...]), 64)
    send_group(gs3, gr3, 1, sum_a[...], 96)
    start(group[3])
    volume(0)
    volume(1)
    received_table(2)
    arrive_halo(halo_m[1])
    middle_halo(1)
    arrive_halo(halo_c)
    receive(2, 0, hr2[0, 0])
    receive(2, 1, hr2[0, 1])
    arrive(group[2])
    mean = take_group(gr2, 0, 32)

    arrive_halo(halo_f[3])
    arrive(group[3])
    fine_halo(3)
    receive(1, 1, take_group(gr3, 0, 0) + start_mc, new=True)
    receive(2, 2, take_group(gr3, 1, 0) + mean, new=True)
    for q in range(9):
        out[q, :, 0:64] = u0[q, 0:35, 0:64]
        out[q, :, 64:192] = u1[q, 0:35, :]
        out[q, :, 192:448] = u2[q, 0:35, :]
    for copies in halo_f + halo_m + [halo_c]:
        pl.when(jnp.logical_not(last))(copies[0].wait_send)
        pl.when(jnp.logical_not(first))(copies[1].wait_send)
    for copies in group:
        for copy in copies:
            copy.wait_send()


def scratch(held):
    shapes = [pltpu.VMEM(x.shape, x.dtype) for x in held]
    shapes += [pltpu.SemaphoreType.DMA((len(held),))]
    shapes += [pltpu.VMEM((9, 40, w), F32) for w in WIDE] * 2
    shapes += [pltpu.VMEM((o // 128, 288, 128), BF16) for o in OWN]
    shapes += [pltpu.VMEM((144, o), F32) for o in OWN]
    shapes += [pltpu.VMEM((9 * w // 128, 144, 128), BF16) for w in WIDE]
    shapes += [pltpu.VMEM((9, 96, 128), BF16)]
    shapes += [pltpu.VMEM((120, 9 * w), F32) for w in WIDE]
    shapes += [pltpu.VMEM((18, 128, 128), BF16)]
    shapes += [pltpu.VMEM((9, 128, 128), BF16)] * 3
    shapes += [pltpu.VMEM((o // 128, o, 128), BF16) for o in OWN]
    shapes += [pltpu.VMEM((w // 128, e, 128), BF16) for e, w in zip(EXT, WIDE)]
    shapes += [pltpu.VMEM((4, e // 128, 16, 128), BF16) for e in EXT]
    shapes += [pltpu.VMEM((16, e), F32) for e in EXT]
    shapes += [pltpu.VMEM((e // 128, 16, 128), jnp.int32) for e in EXT]
    shapes += [pltpu.VMEM((8, w), jnp.int32) for w in WIDE]
    shapes += [pltpu.VMEM((s // 128, o, 128), BF16) for o, s in zip(OWN, SENT)]
    shapes += [pltpu.VMEM((32, w), F32) for w in WIDE]
    shapes += [pltpu.VMEM((1, o), F32) for o in OWN]
    shapes += [pltpu.VMEM((o // 128, 16, 128), jnp.int32) for o in OWN]
    shapes += [pltpu.VMEM((8, w), jnp.int32) for w in WIDE] + [pltpu.VMEM((8, 128), jnp.int32)]
    shapes += [pltpu.VMEM((3, 256, 128), BF16)]
    shapes += [pltpu.VMEM((3, 40, 128), F32), pltpu.VMEM((48, 128), F32)]
    shapes += [pltpu.VMEM((120, 144), BF16)]
    shapes += [pltpu.VMEM((64, 96), BF16), pltpu.VMEM((96, 128), BF16)]
    shapes += [pltpu.VMEM((144, s), F32) for s in SENT]
    shapes += [pltpu.VMEM((144, 128), F32)] * 3
    shapes += [pltpu.VMEM((4, 2, 48, 128), F32)] * 2
    shapes += [pltpu.VMEM((2, 2, 80, 128), F32)] * 2
    shapes += [pltpu.VMEM((1, 2, 144, 128), F32)] * 2
    for buffers in (2, 1, 1, 2, 1):
        shapes += [pltpu.VMEM((N_SUB, 16 * buffers, 128), F32)] * 2
    for slots in (4, 2, 1):
        shapes += [pltpu.SemaphoreType.DMA((slots, 2))] * 2
    shapes += [pltpu.SemaphoreType.DMA((5, 4))] * 2
    return shapes


def solution(mesh):
    n_dom = mesh.shape["dom"]
    place, select, spread, turns = constants()

    def on_device(*arrays):
        held = arrays[:-1] + (
            arrays[-1].transpose(1, 0, 2),
            jnp.asarray(place, BF16), jnp.asarray(select, F32), jnp.asarray(spread, BF16),
            jnp.asarray(turns),
        )
        return pl.pallas_call(
            functools.partial(kernel, n_dom),
            out_shape=pltpu.VMEM(arrays[0].shape, F32),
            in_specs=[pl.BlockSpec(memory_space=pltpu.HBM)] * 14,
            out_specs=pl.BlockSpec(memory_space=pltpu.VMEM),
            scratch_shapes=scratch(held),
            compiler_params=pltpu.CompilerParams(
                collective_id=0, has_side_effects=True, vmem_limit_bytes=60 * 1024 * 1024
            ),
            name="step",
        )(*held)

    split_all = ("dom", "sub")
    placed = (
        P(None, None, split_all), P(None, split_all), P(None, None, split_all),
        P(None, split_all), P(), P(), P(None, split_all), P(None, split_all),
        P(None, split_all), P(None, None, split_all),
    )
    return jax.shard_map(
        on_device, mesh=mesh, in_specs=placed, out_specs=P(None, None, split_all), check_vma=False,
    )
```

```python
import functools

import jax
import jax.numpy as jnp
import numpy as np
from jax import lax
from jax.experimental import pallas as pl
from jax.experimental.pallas import tpu as pltpu
from jax.sharding import PartitionSpec as P

F32 = jnp.float32
BF16 = jnp.bfloat16
MESH = pl.DeviceIdType.MESH
N_SUB = 4
COARSE_STEP = 0.1

LANE = (0, 64, 192)
WIDE = (128, 128, 256)
OWN = (512, 512, 1024)
EXT = (128, 256, 384)
SENT = (128, 256, 256)
STEP = (COARSE_STEP / 4, COARSE_STEP / 2, COARSE_STEP)

VOIGT = ((3, 8, 7), (8, 4, 6), (7, 6, 5))


def face_tables():
    lattice = [
        (a, b, c, 4 - a - b - c) for a in range(5) for b in range(5 - a) for c in range(5 - a - b)
    ]
    face_rows = np.array(
        [[i for i, p in enumerate(lattice) if p[f] == 0] for f in range(4)], np.int32
    )
    triangle = [p[1:] for p in lattice if p[0] == 0]
    position = {p: i for i, p in enumerate(triangle)}

    def turned(p, times):
        p = (p[1], p[0], p[2])
        for _ in range(times):
            p = (p[1], p[2], p[0])
        return p

    orders = np.array(
        [[position[turned(p, o)] for p in triangle] for o in range(3)], np.int32
    )
    return face_rows, orders


def constants():
    face_rows, orders = face_tables()
    place = np.zeros((2, 128, 144), np.float32)
    for n in range(35):
        place[0, n, n] = 1
        place[0, n, 48 + n] = 1
        place[1, n, 96 + n] = 1
    select = np.zeros((128, 144), np.float32)
    for f in range(4):
        for n in range(15):
            select[f * 16 + n, face_rows[f, n]] = 1
            select[64 + f * 16 + n, 48 + face_rows[f, n]] = 1
    spread = np.zeros((2, 128, 128), np.float32)
    for f in range(4):
        for n in range(15):
            spread[0, f * 15 + n, f * 16 + n] = 1
            spread[0, f * 15 + n, 64 + f * 16 + n] = 1
            spread[1, f * 15 + n, f * 16 + n] = 1
    turns = np.full((3, 16, 128), 15, np.int32)
    turns[:, :15] = orders[:, :, None]
    return place, select, spread, turns


def split(x):
    high = x.astype(BF16)
    return high, (x - high.astype(F32)).astype(BF16)


def dot(a, b):
    return jnp.dot(a, b, preferred_element_type=F32)


def lanes(shape):
    return lax.broadcasted_iota(jnp.int32, shape, 1)


def turn(x, shift):
    shift %= 128
    return pltpu.roll(x, shift, 1) if shift else x


def put(ref, rows, tile, value):
    for i in range(value.shape[1] // 128):
        ref[tile + i, rows, :] = value[:, 128 * i : 128 * i + 128]


def get(ref, rows=slice(None), start=0, stop=None):
    stop = ref.shape[0] if stop is None else stop
    return jnp.concatenate([ref[i, rows, :] for i in range(start, stop)], axis=1)


def fill_one_hot(ref, tile, indices, base=0, rows=None):
    chunk = 32
    for start in range(0, rows or ref.shape[1], chunk):
        iota = lax.broadcasted_iota(jnp.int32, (chunk, indices[0].shape[1]), 0)
        hit = None
        for index in indices:
            here = iota == jnp.broadcast_to(index - (base + start), iota.shape)
            hit = here if hit is None else hit | here
        put(ref, slice(start, start + chunk), tile, jnp.where(hit, 1.0, 0.0).astype(BF16))


def kernel(
    n_dom,
    *refs,
):
    ins, out, held, in_sems, rest = refs[:14], refs[14], refs[15:29], refs[29], refs[30:]
    body(n_dom, ins, in_sems, out, *held, *rest)


def body(
    n_dom, ins, in_sems, out,
    wave, mat, geo, fs, der, lift, nbr, ori, halo, iface, place, select, spread, turns,
    u0, u1, u2, v0, v1, v2, t0, t1, t2, g0, g1, g2,
    stack0, stack1, stack2, stack3, prod0, prod1, prod2, jump, xj0, xj1, xj2,
    oh0, oh1, oh2, xx0, xx1, xx2, xm0, xm1, xm2, xs0, xs1, xs2,
    xi0, xi1, xi2, tn0, tn1, tn2,
    os0, os1, os2, cf0, cf1, cf2, sc0, sc1, sc2, om0, om1, om2,
    ix0, ix1, ix2, row_of, xtab, dpad, lpad, amat, emat, lmat, sent0, sent1, sent2, sum_a, sum_b, base0,
    hs0, hr0, hs1, hr1, hs2, hr2, gs0, gr0, gs1, gr1, gs2, gr2, gs3, gr3, gs4, gr4,
    ss0, rs0, ss1, rs1, ss2, rs2, gss, grs,
):
    us, vs, ts, gs_, ohs, oss = (u0, u1, u2), (v0, v1, v2), (t0, t1, t2), (g0, g1, g2), (oh0, oh1, oh2), (os0, os1, os2)
    cfs, scs, oms, sents = (cf0, cf1, cf2), (sc0, sc1, sc2), (om0, om1, om2), (sent0, sent1, sent2)
    prods, stacks, xjs = (prod0, prod1, prod2), (stack0, stack1, stack2), (xj0, xj1, xj2)
    xis, turn_of = (xi0, xi1, xi2), (tn0, tn1, tn2)
    xxs, xms, xss = (xx0, xx1, xx2), (xm0, xm1, xm2), (xs0, xs1, xs2)
    total = n_dom * N_SUB
    dom = lax.axis_index("dom")
    sub = lax.axis_index("sub")
    me = dom * N_SUB + sub
    up = (me + 1) % total
    down = (me + total - 1) % total
    up_id = (up // N_SUB, up % N_SUB)
    down_id = (down // N_SUB, down % N_SUB)
    first, last = me == 0, me == total - 1

    barrier = pltpu.get_barrier_semaphore()

    @pl.when(jnp.logical_not(last))
    def _():
        pl.semaphore_signal(barrier, inc=1, device_id=up_id, device_id_type=MESH)

    @pl.when(jnp.logical_not(first))
    def _():
        pl.semaphore_signal(barrier, inc=1, device_id=down_id, device_id_type=MESH)

    for k in range(1, N_SUB):
        pl.semaphore_signal(
            barrier, inc=1, device_id=(dom, (sub + k) % N_SUB), device_id_type=MESH
        )

    def halo_copies(send, recv, ssem, rsem, slot):
        return [
            pltpu.make_async_remote_copy(
                src_ref=send.at[slot, way], dst_ref=recv.at[slot, way],
                send_sem=ssem.at[slot, way], recv_sem=rsem.at[slot, way],
                device_id=(up_id, down_id)[way], device_id_type=MESH,
            )
            for way in range(2)
        ]

    def group_copies(send, recv, number):
        found = []
        for k in range(1, N_SUB):
            dest = (sub + k) % N_SUB
            found.append(
                pltpu.make_async_remote_copy(
                    src_ref=send.at[dest], dst_ref=recv.at[sub],
                    send_sem=gss.at[number, k], recv_sem=grs.at[number, k],
                    device_id=(dom, dest), device_id_type=MESH,
                )
            )
        return found

    held = (wave, mat, geo, fs, der, lift, nbr, ori, halo, iface, place, select, spread, turns)
    fetch = {
        i: pltpu.make_async_copy(ins[i], held[i], in_sems.at[i])
        for i in (11, 0, 8, 9, 4, 5, 10, 12, 1, 2, 3, 7, 6, 13)
    }
    for copy in fetch.values():
        copy.start()

    def fetched(*numbers):
        for i in numbers:
            fetch[i].wait()

    for end, way in ((first, 0), (last, 1)):

        @pl.when(end)
        def _():
            for ref in (hr0, hr1, hr2):
                ref[:, way] = jnp.zeros((ref.shape[0],) + ref.shape[2:], F32)

    halo_f = [halo_copies(hs0, hr0, ss0, rs0, s) for s in range(4)]
    halo_m = [halo_copies(hs1, hr1, ss1, rs1, s) for s in range(2)]
    halo_c = halo_copies(hs2, hr2, ss2, rs2, 0)
    group = [
        group_copies(s, r, i)
        for i, (s, r) in enumerate(((gs0, gr0), (gs1, gr1), (gs2, gr2), (gs3, gr3), (gs4, gr4)))
    ]

    fetched(11)
    emat[...] = (select[0:64, 0:96] + select[64:128, 0:96]).astype(BF16)

    def matrices():
        dpad[...] = jnp.zeros_like(dpad)
        lpad[...] = jnp.zeros_like(lpad)
        fetched(4, 5, 10, 12)
        for k in range(3):
            dpad[k, 0:35, 0:35] = der[k]
        lpad[0:35, 0:60] = lift[...]
        parts = []
        for k in range(3):
            high, low = split(dpad[k])
            parts.append(dot(high, place[0]) + dot(low, place[1]))
        amat[...] = jnp.concatenate(parts, axis=0).astype(BF16)
        high, low = split(lpad[...])
        lmat[0:48] = dot(high, spread[0]).astype(BF16)
        lmat[48:96] = dot(low, spread[1]).astype(BF16)

    def remap(index, c):
        if c:
            return index
        return jnp.where(
            index < 256, (index & 63) + ((index >> 6) << 7), index + 256
        )

    def order_of(turned):
        return jnp.where(turned == 0, turns[0], jnp.where(turned == 1, turns[1], turns[2]))

    def reorder(x, order):
        found = []
        for half in (order[0:8], order[8:16]):
            row = half & 7
            low = jnp.take_along_axis(x[0:8], row, axis=0, mode="promise_in_bounds")
            high = jnp.take_along_axis(x[8:16], row, axis=0, mode="promise_in_bounds")
            found.append(jnp.where(half < 8, low, high))
        return jnp.concatenate(found, axis=0)

    def load(c):
        first, wide = LANE[c], WIDE[c]
        span = slice(first, first + wide)
        u = us[c]
        for q in range(9):
            u[q, 32:40, :] = jnp.zeros((8, wide), F32)
            u[q, 0:35, :] = wave[q, :, span]

    def coefficients(c):
        first, wide = LANE[c], WIDE[c]
        span = slice(first, first + wide)
        rho = STEP[c] / mat[0:1, span]
        lam = STEP[c] * mat[1:2, span]
        mu = STEP[c] * mat[2:3, span]
        cf = cfs[c]
        for i in range(3):
            axes = geo[i, :, span]
            cf[3 * i : 3 * i + 3] = axes * mu
            cf[9 + 3 * i : 12 + 3 * i] = axes * rho
            cf[18 + 3 * i : 21 + 3 * i] = axes
        cf[27:28] = lam
        cf[28:29] = 2.0 * mu
        for f in range(4):
            where = slice(f * wide, (f + 1) * wide)
            scs[c][:, where] = (0.5 * STEP[c]) * fs[f : f + 1, span]
            turn_of[c][f : f + 1] = ori[f : f + 1, span]
            for j in range(wide // 128):
                oms[c][f * wide // 128 + j] = order_of(
                    jnp.broadcast_to(turn_of[c][f : f + 1, 128 * j : 128 * j + 128], (16, 128))
                )

    def send_table(c):
        blank = jnp.full((1, 64), -1, jnp.int32)
        if c == 0:
            rows = [(halo[0:1, 0:32], halo[1:2, 0:32], iface[0, 0:1], iface[1, 0:1])]
        elif c == 1:
            rows = [(halo[0:1, 32:96], halo[1:2, 32:96]), (iface[0, 1:2], iface[2, 0:1], blank)]
        else:
            rows = [(halo[0:1, 96:224],), (halo[1:2, 96:224],)]
        for i, row in enumerate(rows):
            at = slice(3 * c + i, 3 * c + i + 1)
            row_of[at] = remap(jnp.concatenate(row, axis=1), c)
            fill_one_hot(oss[c], i, [row_of[at]])

    def neighbour_table(c):
        wide, own = WIDE[c], OWN[c]
        span = slice(LANE[c], LANE[c] + wide)
        index = remap(nbr[:, span], c)
        if c == 0:
            index = jnp.where(lanes(index.shape) < 64, index, -1)
        ixs = (ix0, ix1, ix2)[c]
        ixs[...] = jnp.full((8, wide), -1, jnp.int32)
        ixs[0:4] = index
        for f in range(4):
            fill_one_hot(ohs[c], f * wide // 128, [ixs[f : f + 1]])

    def received_table(c):
        wide, own, ext = WIDE[c], OWN[c], EXT[c]
        ixs = (ix0, ix1, ix2)[c]
        upright = (ixs[...] - own).astype(F32).T
        across = lanes((32, ext)).astype(F32)
        scale_at, turned_at = None, None
        for f in range(4):
            face = slice(f * wide, (f + 1) * wide)
            high, low = split(jnp.broadcast_to(scs[c][:, face], (16, wide)))
            turned = jnp.broadcast_to(turn_of[c][f : f + 1].astype(F32), (16, wide)).astype(BF16)
            tall = jnp.concatenate([turned, jnp.ones((16, wide), BF16), high, low], axis=0)
            for start in range(0, wide, 32):
                column = jnp.broadcast_to(upright[start : start + 32, f : f + 1], (32, ext))
                put(xtab, slice(start, start + 32), 0, jnp.where(column == across, 1.0, 0.0).astype(BF16))
            found = dot(tall, get(xtab, slice(0, wide), 0, ext // 128))
            put(xms[c].at[f], slice(None), 0, found[16:32].astype(BF16))
            both = found[32:48] + found[48:64]
            scale_at = both if scale_at is None else scale_at + both
            turned_at = found[0:16] if turned_at is None else turned_at + found[0:16]
        for i in range(ext // 128):
            xis[c][i] = order_of(turned_at[:, 128 * i : 128 * i + 128].astype(jnp.int32))
        fill_one_hot(xxs[c], 0, [ixs[f : f + 1] for f in range(4)], own)
        xss[c][...] = scale_at

    def early(c, row):
        wide = WIDE[c]
        at = slice(2 * c - 1, 2 * c)
        row_of[at] = row
        row = row_of[at]
        element, face = row & (wide - 1), row >> (7 if c == 1 else 8)
        tall = jnp.concatenate([us[c][q] for q in range(9)], axis=0)
        high = tall.astype(BF16).astype(F32)
        both = jnp.concatenate([high, tall - high], axis=1).astype(BF16)
        fill_one_hot(xtab, 0, [element], rows=wide)
        columns = xtab[0, 0:wide]
        picked = dot(both, jnp.concatenate([columns, columns], axis=0))
        gap = jnp.zeros((8, 128), F32)
        for q in range(9):
            x = picked[40 * q : 40 * q + 40]
            high = x.astype(BF16).astype(F32)
            pair = [high, gap, x - high, gap]
            stack3[q] = jnp.concatenate(pair, axis=0).astype(BF16)
        nodes = dot(emat[...], get(stack3))
        face = jnp.broadcast_to(face, (16, 128))
        found = []
        for q in range(9):
            span = slice(128 * q, 128 * q + 128)
            acc = jnp.zeros((16, 128), F32)
            for f in range(4):
                acc = jnp.where(face == f, nodes[16 * f : 16 * f + 16, span], acc)
            found.append(acc)
        return jnp.concatenate(found, axis=0)

    def traces(c):
        wide = WIDE[c]
        u, t, stack = us[c], ts[c], stacks[c]
        gap = jnp.zeros((8, wide), F32)
        for q in range(9):
            x = u[q]
            high = x.astype(BF16).astype(F32)
            tall = jnp.concatenate([high, gap, x - high, gap, high, gap], axis=0)
            put(stack, slice(None), q * wide // 128, tall.astype(BF16))
        picked = dot(emat[...], get(stack, slice(0, 96)))
        for q in range(9):
            where = slice(q * wide, (q + 1) * wide)
            for f in range(4):
                at, tile = 16 * q, f * wide // 128
                high, low = split(picked[16 * f : 16 * f + 16, where])
                put(t, slice(at, at + 16), tile, high)
                put(t, slice(144 + at, 160 + at), tile, low)
        both = dot(get(t), get(oss[c]))
        sents[c][...] = both[0:144] + both[144:288]

    def volume(c):
        wide = WIDE[c]
        cf, prod, t = cfs[c], prods[c], ts[c]
        tiles, own_tiles = wide // 128, OWN[c] // 128
        prod[...] = dot(amat[...], get(stacks[c]))
        both = dot(get(t), get(ohs[c]))
        gs_[c][...] = both[0:144] + both[144:288]
        scale = scs[c][...]
        for j in range(own_tiles):
            lane = slice(128 * j, 128 * j + 128)
            f, part = j // tiles, j % tiles
            order = oms[c][j]
            for q in range(9):
                at = 16 * q
                outer = reorder(gs_[c][at : at + 16, lane], order)
                mine = t[j, at : at + 16].astype(F32) + t[j, 144 + at : 160 + at].astype(F32)
                high, low = split((outer - mine) * scale[:, lane])
                jump[q * tiles + part, 16 * f : 16 * f + 16] = high
                jump[q * tiles + part, 64 + 16 * f : 80 + 16 * f] = low
        first = dot(lmat[...], get(jump, slice(None), 0, 9 * tiles))
        whole = first[0:40] + first[48:88]
        for start in range(0, wide, 128):
            span = slice(start, start + 128)

            def old(q):
                at = q * wide + start
                return us[c][q, :, span] + whole[:, at : at + 128]

            def grad(q, i, kind):
                at = q * wide + start
                base = 9 * kind + 3 * i
                return sum(
                    jnp.broadcast_to(cf[base + k : base + k + 1, span], (40, 128))
                    * prod[40 * k : 40 * k + 40, at : at + 128]
                    for k in range(3)
                )

            for i in range(3):
                rate = grad(VOIGT[i][0], 0, 1) + grad(VOIGT[i][1], 1, 1) + grad(VOIGT[i][2], 2, 1)
                vs[c][i, :, span] = old(i) + rate
            diag = [grad(i, i, 2) for i in range(3)]
            shared = cf[27:28, span] * (diag[0] + diag[1] + diag[2])
            for i in range(3):
                vs[c][3 + i, :, span] = old(3 + i) + (shared + cf[28:29, span] * diag[i])
            for q, i, j in ((6, 1, 2), (7, 0, 2), (8, 0, 1)):
                rate = grad(j, i, 0) + grad(i, j, 0)
                vs[c][q, :, span] = old(q) + rate

    def receive(c, tile, value, new=False):
        span = slice(128 * tile, 128 * tile + 128)
        xj = xjs[c]
        scale, order = xss[c][:, span], xis[c][tile]
        for q in range(9):
            high, low = split(reorder(value[16 * q : 16 * q + 16], order) * scale)
            for f in range(4):
                mask = xms[c][f, tile]
                xj[q, 16 * f : 16 * f + 16] = high * mask
                xj[q, 64 + 16 * f : 80 + 16 * f] = low * mask
        first = dot(lmat[...], get(xj))
        whole = first[0:40] + first[48:88]
        tall = jnp.concatenate([whole[:, 128 * q : 128 * q + 128] for q in range(9)], axis=0)
        high = tall.astype(BF16).astype(F32)
        both = jnp.concatenate([high, tall - high], axis=1).astype(BF16)
        columns = get(xxs[c], span)
        added = dot(both, jnp.concatenate([columns, columns], axis=0))
        target = us[c] if new else vs[c]
        for q in range(9):
            at = 40 * q
            target[q] = vs[c][q] + added[at : at + 40]

    lane48 = lanes((48, 128))
    lane16 = lanes((16, 128))

    def pack_third(x, base):
        return jnp.where(
            lane48 < 32, turn(x[0:48], -base),
            jnp.where(lane48 < 64, turn(x[48:96], 32 - base), turn(x[96:144], 64 - base)),
        )

    def send_fine(slot):
        x = sent0[...]
        hs0[slot, 0] = pack_third(x, 32)
        hs0[slot, 1] = pack_third(x, 0)

    def send_middle(slot):
        x = sent1[:, 0:128]
        lower = x[0:80]
        upper = jnp.concatenate([x[80:144], jnp.zeros((16, 128), F32)], axis=0)
        left = lanes((80, 128)) < 64
        hs1[slot, 0] = jnp.where(left, turn(lower, 64), upper)
        hs1[slot, 1] = jnp.where(left, lower, turn(upper, 64))

    def send_group(send, recv, number, x, base):
        rows = slice(16 * number, 16 * number + 16)
        for j in range(N_SUB):
            acc = jnp.zeros((16, 128), F32)
            for q in range(9):
                piece = turn(x[16 * q : 16 * q + 16], 8 * q - base - 8 * j)
                acc = jnp.where((lane16 >= 8 * q) & (lane16 < 8 * q + 8), piece, acc)
            send[j, rows] = acc
        recv[sub, rows] = send[sub, rows]

    def take_group(recv, number, base):
        rows = slice(16 * number, 16 * number + 16)
        pieces = [recv[p, rows] for p in range(N_SUB)]
        found = []
        for q in range(9):
            acc = jnp.zeros((16, 128), F32)
            for p in range(N_SUB):
                at = base + 8 * p
                acc = jnp.where(
                    (lane16 >= at) & (lane16 < at + 8), turn(pieces[p], at - 8 * q), acc
                )
            found.append(acc)
        return jnp.concatenate(found, axis=0)

    def start(copies):
        for copy in copies:
            copy.start()

    def arrive(copies):
        for copy in copies:
            copy.wait_recv()

    def start_halo(copies):
        pl.when(jnp.logical_not(last))(copies[0].start)
        pl.when(jnp.logical_not(first))(copies[1].start)

    def arrive_halo(copies):
        pl.when(jnp.logical_not(first))(copies[0].wait_recv)
        pl.when(jnp.logical_not(last))(copies[1].wait_recv)

    def fine_halo(slot):
        below = hr0[slot, 0]
        above = hr0[slot, 1]
        found = []
        for r in range(3):
            found.append(
                jnp.where(
                    lane48 < 32, turn(below, -32 * r),
                    jnp.where(lane48 < 64, turn(above, 32 - 32 * r), base0[48 * r : 48 * r + 48]),
                )
            )
        receive(0, 0, jnp.concatenate(found, axis=0), new=True)

    def middle_halo(slot):
        below = hr1[slot, 0]
        above = hr1[slot, 1]
        left = lanes((80, 128)) < 64
        lower = jnp.where(left, below, turn(above, 64))
        upper = jnp.where(left, turn(below, 64), above)
        receive(1, 0, jnp.concatenate([lower, upper[0:64]], axis=0))

    fetched(0, 8, 9)
    load(0)
    send_table(0)
    traces(0)
    sum_a[...] = sent0[...]
    send_fine(0)
    pl.semaphore_wait(barrier, N_SUB - 1 + (me + total - 1) // total + 1 - (me + 1) // total)
    start_halo(halo_f[0])
    load(1)
    load(2)
    blank = jnp.full((1, 64), -1, jnp.int32)
    start_m = early(1, jnp.concatenate([iface[0, 1:2], iface[2, 0:1], blank], axis=1))
    start_c = early(2, jnp.concatenate([iface[1, 1:2], iface[2, 1:2], blank], axis=1))
    sum_b[...] = start_m
    send_group(gs0, gr0, 0, start_m, 0)
    send_group(gs0, gr0, 1, start_c, 0)
    start(group[0])
    send_group(gs4, gr4, 0, start_c, 32)
    start(group[4])
    send_table(1)
    traces(1)
    send_middle(0)
    start_halo(halo_m[0])
    send_table(2)
    traces(2)
    hs2[0, 0] = sent2[:, 128:256]
    hs2[0, 1] = sent2[:, 0:128]
    start_halo(halo_c)
    matrices()
    fetched(1, 2, 3, 7, 6, 13)
    coefficients(0)
    neighbour_table(0)
    received_table(0)
    volume(0)
    coefficients(1)
    coefficients(2)
    neighbour_table(1)
    received_table(1)
    arrive(group[0])
    base0[...] = take_group(gr0, 0, 64) + take_group(gr0, 1, 96)

    arrive_halo(halo_f[0])
    fine_halo(0)
    traces(0)
    send_fine(1)
    start_halo(halo_f[1])
    sum_a[...] += sent0[...]
    send_group(gs1, gr1, 0, 0.5 * sum_a[...], 64)
    start(group[1])
    volume(0)
    volume(1)
    arrive_halo(halo_m[0])
    middle_halo(0)
    arrive(group[4])
    start_mc = take_group(gr4, 0, 32)
    neighbour_table(2)

    arrive_halo(halo_f[1])
    fine_halo(1)
    traces(0)
    send_fine(2)
    start_halo(halo_f[2])
    sum_a[...] = 0.25 * sum_a[...] + 0.25 * sent0[...]
    base1 = sent0[...]
    volume(0)

    arrive(group[1])
    receive(1, 1, take_group(gr1, 0, 0) + start_mc, new=True)
    traces(1)
    send_middle(1)
    start_halo(halo_m[1])
    send_group(gs2, gr2, 0, 0.5 * (sum_b[...] + sent1[:, 128:256]), 32)
    start(group[2])
    volume(2)

    arrive_halo(halo_f[2])
    fine_halo(2)
    traces(0)
    send_fine(3)
    start_halo(halo_f[3])
    sum_a[...] += 0.25 * sent0[...]
    send_group(gs3, gr3, 0, 0.5 * (base1 + sent0[...]), 64)
    send_group(gs3, gr3, 1, sum_a[...], 96)
    start(group[3])
    volume(0)
    volume(1)
    received_table(2)
    arrive_halo(halo_m[1])
    middle_halo(1)
    arrive_halo(halo_c)
    receive(2, 0, hr2[0, 0])
    receive(2, 1, hr2[0, 1])
    arrive(group[2])
    mean = take_group(gr2, 0, 32)

    arrive_halo(halo_f[3])
    arrive(group[3])
    fine_halo(3)
    receive(1, 1, take_group(gr3, 0, 0) + start_mc, new=True)
    receive(2, 2, take_group(gr3, 1, 0) + mean, new=True)
    for q in range(9):
        out[q, :, 0:64] = u0[q, 0:35, 0:64]
        out[q, :, 64:192] = u1[q, 0:35, :]
        out[q, :, 192:448] = u2[q, 0:35, :]
    for copies in halo_f + halo_m + [halo_c]:
        pl.when(jnp.logical_not(last))(copies[0].wait_send)
        pl.when(jnp.logical_not(first))(copies[1].wait_send)
    for copies in group:
        for copy in copies:
            copy.wait_send()


def scratch(held):
    shapes = [pltpu.VMEM(x.shape, x.dtype) for x in held]
    shapes += [pltpu.SemaphoreType.DMA((len(held),))]
    shapes += [pltpu.VMEM((9, 40, w), F32) for w in WIDE] * 2
    shapes += [pltpu.VMEM((o // 128, 288, 128), BF16) for o in OWN]
    shapes += [pltpu.VMEM((144, o), F32) for o in OWN]
    shapes += [pltpu.VMEM((9 * w // 128, 144, 128), BF16) for w in WIDE]
    shapes += [pltpu.VMEM((9, 96, 128), BF16)]
    shapes += [pltpu.VMEM((120, 9 * w), F32) for w in WIDE]
    shapes += [pltpu.VMEM((18, 128, 128), BF16)]
    shapes += [pltpu.VMEM((9, 128, 128), BF16)] * 3
    shapes += [pltpu.VMEM((o // 128, o, 128), BF16) for o in OWN]
    shapes += [pltpu.VMEM((w // 128, e, 128), BF16) for e, w in zip(EXT, WIDE)]
    shapes += [pltpu.VMEM((4, e // 128, 16, 128), BF16) for e in EXT]
    shapes += [pltpu.VMEM((16, e), F32) for e in EXT]
    shapes += [pltpu.VMEM((e // 128, 16, 128), jnp.int32) for e in EXT]
    shapes += [pltpu.VMEM((8, w), jnp.int32) for w in WIDE]
    shapes += [pltpu.VMEM((s // 128, o, 128), BF16) for o, s in zip(OWN, SENT)]
    shapes += [pltpu.VMEM((32, w), F32) for w in WIDE]
    shapes += [pltpu.VMEM((1, o), F32) for o in OWN]
    shapes += [pltpu.VMEM((o // 128, 16, 128), jnp.int32) for o in OWN]
    shapes += [pltpu.VMEM((8, w), jnp.int32) for w in WIDE] + [pltpu.VMEM((8, 128), jnp.int32)]
    shapes += [pltpu.VMEM((3, 256, 128), BF16)]
    shapes += [pltpu.VMEM((3, 40, 128), F32), pltpu.VMEM((48, 128), F32)]
    shapes += [pltpu.VMEM((120, 144), BF16)]
    shapes += [pltpu.VMEM((64, 96), BF16), pltpu.VMEM((96, 128), BF16)]
    shapes += [pltpu.VMEM((144, s), F32) for s in SENT]
    shapes += [pltpu.VMEM((144, 128), F32)] * 3
    shapes += [pltpu.VMEM((4, 2, 48, 128), F32)] * 2
    shapes += [pltpu.VMEM((2, 2, 80, 128), F32)] * 2
    shapes += [pltpu.VMEM((1, 2, 144, 128), F32)] * 2
    for buffers in (2, 1, 1, 2, 1):
        shapes += [pltpu.VMEM((N_SUB, 16 * buffers, 128), F32)] * 2
    for slots in (4, 2, 1):
        shapes += [pltpu.SemaphoreType.DMA((slots, 2))] * 2
    shapes += [pltpu.SemaphoreType.DMA((5, 4))] * 2
    return shapes


def solution(mesh):
    n_dom = mesh.shape["dom"]
    place, select, spread, turns = constants()

    def on_device(*arrays):
        held = arrays[:-1] + (
            arrays[-1].transpose(1, 0, 2),
            jnp.asarray(place, BF16), jnp.asarray(select, F32), jnp.asarray(spread, BF16),
            jnp.asarray(turns),
        )
        return pl.pallas_call(
            functools.partial(kernel, n_dom),
            out_shape=pltpu.VMEM(arrays[0].shape, F32),
            in_specs=[pl.BlockSpec(memory_space=pltpu.HBM)] * 14,
            out_specs=pl.BlockSpec(memory_space=pltpu.VMEM),
            scratch_shapes=scratch(held),
            compiler_params=pltpu.CompilerParams(
                collective_id=0, has_side_effects=True, vmem_limit_bytes=60 * 1024 * 1024
            ),
            name="step",
        )(*held)

    split_all = ("dom", "sub")
    placed = (
        P(None, None, split_all), P(None, split_all), P(None, None, split_all),
        P(None, split_all), P(), P(), P(None, split_all), P(None, split_all),
        P(None, split_all), P(None, None, split_all),
    )
    return jax.shard_map(
        on_device, mesh=mesh, in_specs=placed, out_specs=P(None, None, split_all), check_vma=False,
    )
```
